32 devices in a mesh: dp: 8 (over z, x), seq: 4 (over y, core).
Axes of the slice: x: 2, y: 2, z: 4, core: 2. Of those that a mesh axis runs over, the one named last changes fastest.
Arguments:
- tokens: bfloat16 [2, 8, 1024, 1024], P(None, 'dp', 'seq'), may hold values from -6 to 6
- segment_ids: int32 [2, 8, 1024], P(None, 'dp', 'seq'), may hold values from 0 to 15, never falling along the last dimension, each value on 1 to 512 neighbouring positions
- cotangent: bfloat16 [2, 8, 1024, 1024], P(None, 'dp', 'seq'), may hold values from -6 to 6
- query_proj: bfloat16 [1024, 1024], P(('dp', 'seq')), may hold values from -0.1875 to 0.1875
- key_proj: bfloat16 [1024, 1024], P(('dp', 'seq')), may hold values from -0.1875 to 0.1875
- value_proj: bfloat16 [1024, 1024], P(('dp', 'seq')), may hold values from -0.1875 to 0.1875
- out_proj: bfloat16 [1024, 1024], P(('dp', 'seq')), may hold values from -0.5 to 0.5
- value_bias: bfloat16 [1024], P(('dp', 'seq')), may hold values from -3 to 3
- content_bias: bfloat16 [1024], P(('dp', 'seq')), may hold values from -3 to 3
- position_bias: bfloat16 [1024], P(('dp', 'seq')), may hold values from -3 to 3
- position_proj: bfloat16 [1024, 64], P(('dp', 'seq')), may hold values from -0.75 to 0.75
- out_bias: bfloat16 [1024], P(('dp', 'seq')), may hold values from -3 to 3
- attn_gain: bfloat16 [1024], P(('dp', 'seq')), may hold values from 0.5 to 1.5
- attn_shift: bfloat16 [1024], P(('dp', 'seq')), may hold values from -2 to 2
- inner_proj: bfloat16 [1024, 4096], P(('dp', 'seq')), may hold values from -0.1875 to 0.1875
- inner_bias: bfloat16 [4096], P(('dp', 'seq')), may hold values from -3 to 3
- outer_proj: bfloat16 [4096, 1024], P(('dp', 'seq')), may hold values from -0.1875 to 0.1875
- outer_bias: bfloat16 [1024], P(('dp', 'seq')), may hold values from -2 to 2
- final_gain: bfloat16 [1024], P(('dp', 'seq')), may hold values from 0.5 to 1.5
- final_shift: bfloat16 [1024], P(('dp', 'seq')), may hold values from -2 to 2
Outputs:
- output: bfloat16 [2, 8, 1024, 1024], P(None, 'dp', 'seq')
- input_grad: float32 [2, 8, 1024, 1024], P(None, 'dp', 'seq')
- query_proj_grad: float32 [1024, 1024], P(('dp', 'seq'))
- key_proj_grad: float32 [1024, 1024], P(('dp', 'seq'))
- value_proj_grad: float32 [1024, 1024], P(('dp', 'seq'))
- out_proj_grad: float32 [1024, 1024], P(('dp', 'seq'))
- value_bias_grad: float32 [1024], P(('dp', 'seq'))
- content_bias_grad: float32 [1024], P(('dp', 'seq'))
- position_bias_grad: float32 [1024], P(('dp', 'seq'))
- position_proj_grad: float32 [1024, 64], P(('dp', 'seq'))
- out_bias_grad: float32 [1024], P(('dp', 'seq'))
- attn_gain_grad: float32 [1024], P(('dp', 'seq'))
- attn_shift_grad: float32 [1024], P(('dp', 'seq'))
- inner_proj_grad: float32 [1024, 4096], P(('dp', 'seq'))
- inner_bias_grad: float32 [4096], P(('dp', 'seq'))
- outer_proj_grad: float32 [4096, 1024], P(('dp', 'seq'))
- outer_bias_grad: float32 [1024], P(('dp', 'seq'))
- final_gain_grad: float32 [1024], P(('dp', 'seq'))
- final_shift_grad: float32 [1024], P(('dp', 'seq'))
The draws below stay inside these ranges and needn't reach their ends.
Inputs may be any that keep to these rules, and one draw needn't show every extreme that they name: `segment_ids`: ids never fall along a sequence; a token attends to the tokens of its own sequence with the same id.
All inputs are finite; a program needn't handle non-finite values.
Results may differ from the reference program's by a relative error of at most 0.024.
Values may be sent and summed in bfloat16 or wider, within the bound.
No kernel may reach another device: no remote copies, remote signals or barrier semaphores. Data moves between devices by JAX's collectives and lax.ppermute only.
A program may use at most 256 MiB of HBM per device.

```python
import math
import jax
import jax.numpy as jnp
import numpy as np
from jax import lax

H = 16
DH = 64
D = 1024
FF = 4096
SEQ_LEN = 1024
MICRO = 2
SEQS = 8
DOCS = 16
MOST = 512


def raised(array, rng, source, target, parts, factor):
    def block_of(dim):
        return (jnp.arange(array.shape[dim]) // (array.shape[dim] // parts)).reshape((-1,) + (1,) * (array.ndim - 1 - dim))

    one_side = jax.random.permutation(rng, parts)[block_of(target)]
    second = (block_of(target) + parts // 2) % parts
    return jnp.where((block_of(source) == one_side) | (block_of(source) == second), factor * array, array)


def block_scale(key, extent, pieces, least, largest):
    def one(dim, shards_of):
        steps = jax.random.uniform(jax.random.fold_in(jax.random.fold_in(key, 6), dim), (shards_of,), jnp.float32, least / len(pieces), largest / len(pieces))
        return jnp.repeat(jnp.exp(steps), extent[dim] // shards_of).reshape((-1,) + (1,) * (len(extent) - dim - 1))

    loudness = one(*pieces[0])
    for cut in pieces[1:]:
        loudness = loudness * one(*cut)
    return loudness


def length_profile(count, total, limit, slope):
    weights = [(1 << 20) // math.isqrt(grade ** slope) + 1 for grade in range(2, count + 1)]
    rest, holding = total - limit - (count - 1), [1] * (count - 1)
    while rest > 0:
        free = [i for i in range(count - 1) if holding[i] < limit]
        pool, budget = sum([weights[i] for i in free]), rest
        for i in free:
            addition = min(limit - holding[i], max(1, budget * weights[i] // pool), rest)
            holding[i] = holding[i] + addition
            rest = rest - addition
    return np.array([limit] + holding)


def ragged_sizes(stream_key, count, total, bound, skew):
    if count == 2:
        one = jax.random.randint(stream_key, (), max(1, total - bound), min(bound, total - 1) + 1)
        return jnp.stack([one, total - one])
    tallies = jnp.asarray(length_profile(count, total, bound, skew), jnp.int32)
    twos = (count - 1) // 2
    source_of, taker = tallies[1:1 + 2 * twos:2], tallies[2:2 + 2 * twos:2]
    room = jnp.minimum(source_of - 1, bound - taker)
    shifted = jax.random.randint(jax.random.fold_in(stream_key, 1), (twos,), 0, 1 << 20) % (room + 1)
    tallies = tallies.at[1:1 + 2 * twos:2].set(source_of - shifted).at[2:2 + 2 * twos:2].set(taker + shifted)
    return tallies[jax.random.permutation(jax.random.fold_in(stream_key, 2), count)]


def gaussian(rng, extent, deviation, most, pieces=(), kind=jnp.bfloat16):
    values = jax.random.normal(rng, extent, jnp.float32) * deviation
    if len(pieces) > 0:
        values = block_scale(rng, extent, pieces, -0.22, 0.18) * values
    return jnp.clip(values, min=-most, max=most).astype(kind)


def bell_draw_with(rng, dims, scale, limit, shards, heavy, kind=jnp.bfloat16):
    values = scale * jax.random.normal(rng, dims, jnp.float32)
    if shards:
        values = values * block_scale(rng, dims, shards, -0.22, 0.18)
    return jnp.clip(raised(values, jax.random.fold_in(rng, 3), *heavy), -limit, limit).astype(kind)


def setup_inputs(seed: int = 0) -> dict:
    key_list = jax.random.split(jax.random.key(seed), 21)
    tokens = bell_draw_with(key_list[0], (MICRO, SEQS, SEQ_LEN, D), 1.0, 6.0, ((1, 8), (2, 4)), (1, 3, 8, 2.0))
    segment_ids = jax.vmap(lambda own: jnp.searchsorted(jnp.cumsum(ragged_sizes(own, DOCS, SEQ_LEN, MOST, 2)), jnp.arange(SEQ_LEN), side="right"))(jax.random.split(key_list[1], MICRO * SEQS)).reshape((MICRO, SEQS, SEQ_LEN)).astype(jnp.int32)
    cotangent = gaussian(key_list[2], (MICRO, SEQS, SEQ_LEN, D), 1.0, 6.0, ((1, 8), (2, 4)))
    query_proj = gaussian(key_list[3], (D, D), D ** -0.5, 0.1875, ((0, 32),))
    key_proj = gaussian(key_list[4], (D, D), D ** -0.5, 0.1875, ((0, 32),))
    value_proj = gaussian(key_list[5], (D, D), D ** -0.5, 0.1875, ((0, 32),))
    out_proj = gaussian(key_list[6], (D, D), (D // 8) ** -0.5, 0.5, ((0, 32),))
    value_bias = gaussian(key_list[7], (D,), 0.5, 3.0, ((0, 32),))
    content_bias = gaussian(key_list[8], (D,), 0.5, 3.0, ((0, 32),))
    position_bias = gaussian(key_list[9], (D,), 0.5, 3.0, ((0, 32),))
    position_proj = gaussian(key_list[10], (D, DH), DH ** -0.5, 0.75, ((0, 32),))
    out_bias = gaussian(key_list[11], (D,), 0.5, 3.0, ((0, 32),))
    attn_gain = jnp.clip(1.0 + 0.1 * jax.random.normal(key_list[12], (D,), jnp.float32), 0.5, 1.5).astype(jnp.bfloat16)
    attn_shift = gaussian(key_list[13], (D,), 0.3, 2.0, ((0, 32),))
    inner_proj = gaussian(key_list[14], (D, FF), D ** -0.5, 0.1875, ((0, 32),))
    inner_bias = gaussian(key_list[15], (FF,), 0.5, 3.0, ((0, 32),))
    outer_proj = gaussian(key_list[16], (FF, D), (FF // 4) ** -0.5, 0.1875, ((0, 32),))
    outer_bias = gaussian(key_list[17], (D,), 0.3, 2.0, ((0, 32),))
    final_gain = jnp.clip(1.0 + 0.1 * jax.random.normal(key_list[18], (D,), jnp.float32), 0.5, 1.5).astype(jnp.bfloat16)
    final_shift = gaussian(key_list[19], (D,), 0.3, 2.0, ((0, 32),))
    return dict(tokens=tokens, segment_ids=segment_ids, cotangent=cotangent, query_proj=query_proj, key_proj=key_proj, value_proj=value_proj, out_proj=out_proj, value_bias=value_bias, content_bias=content_bias, position_bias=position_bias, position_proj=position_proj, out_bias=out_bias, attn_gain=attn_gain, attn_shift=attn_shift, inner_proj=inner_proj, inner_bias=inner_bias, outer_proj=outer_proj, outer_bias=outer_bias, final_gain=final_gain, final_shift=final_shift)


highest = lax.Precision.HIGHEST

@jax.custom_vjp
def low(v):
    return lax.optimization_barrier(v.astype(jnp.bfloat16)).astype(jnp.float32)

@jax.custom_vjp
def low_back(v):
    return v

def low_keep(v):
    return (low(v), None)

def low_pass(kept, grad):
    return (grad,)

def back_keep(v):
    return (v, None)

def back_low(kept, grad):
    return (low(grad),)
low.defvjp(low_keep, low_pass)
low_back.defvjp(back_keep, back_low)

def rotations(length, half_size):
    position = jnp.arange(length, dtype=jnp.int32).astype(jnp.float32)
    steps = jnp.arange(half_size, dtype=jnp.int32).astype(jnp.float32)
    frequency = jnp.exp(steps * (-math.log(10000.0) / half_size))
    angle = position[:, None] * frequency[None, :]
    return (jnp.cos(angle), jnp.sin(angle))

def layer_norm(values, gain, shift):
    average = lax.optimization_barrier(jnp.mean(values, axis=-1, keepdims=True))
    centred = values - average
    variance = lax.optimization_barrier(jnp.mean(centred * centred, axis=-1, keepdims=True))
    return centred * lax.rsqrt(variance + 1e-06) * gain + shift

def matmul(left, right):
    return jnp.dot(left, right, precision=highest)

def forward(weights, rows, doc_ids):
    query_proj, key_proj, value_proj, out_proj, value_bias, content_bias, position_bias, position_proj, out_bias, attn_gain, attn_shift, inner_proj, inner_bias, outer_proj, outer_bias, final_gain, final_shift = weights
    length = rows.shape[0]
    half_size = DH // 2
    score_scale = DH ** (-0.5)
    queries = low(low_back(matmul(rows, query_proj))).reshape(length, H, DH)
    keys_in = low(low_back(matmul(rows, key_proj))).reshape(length, H, DH)
    values_in = low(low_back(matmul(rows, value_proj))).reshape(length, H, DH)
    cos_table, sin_table = rotations(length, half_size)
    cos_rows = cos_table[:, None, :]
    sin_rows = sin_table[:, None, :]
    q_content = low(queries + content_bias.reshape(H, DH))
    q_pos = low(queries + position_bias.reshape(H, DH))
    turned = jnp.einsum('thd,hdf->thf', q_pos, position_proj.reshape(H, DH, DH), precision=highest)
    turn_cos = turned[..., :half_size]
    turn_sin = turned[..., half_size:]
    q_rel = low(jnp.concatenate([turn_cos * cos_rows + turn_sin * sin_rows, turn_cos * sin_rows - turn_sin * cos_rows], -1))
    key_rel = low(jnp.concatenate([cos_table, sin_table], -1))
    q_full = jnp.concatenate([q_content, q_rel], -1)
    k_full = jnp.concatenate([keys_in, jnp.broadcast_to(key_rel[:, None, :], (length, H, DH))], -1)
    row_block = 512 if length % 512 == 0 else length
    block_count = length // row_block

    def attend_block(block_items):
        q_block, doc_block = block_items
        raw_scores = jnp.einsum('qhd,khd->hqk', q_block, k_full, precision=highest) * score_scale
        scores = low_back(raw_scores)
        same_doc = doc_block[:, None] == doc_ids[None, :]
        probs_full = jax.nn.softmax(jnp.where(same_doc[None], scores, -1e+30), axis=-1)
        return jnp.einsum('hqk,khd->qhd', low(probs_full), values_in, precision=highest)
    mixed_rows = lax.map(jax.checkpoint(attend_block), (q_full.reshape(block_count, row_block, H, 2 * DH), doc_ids.reshape(block_count, row_block)))
    context = low(low_back(mixed_rows.reshape(length, H, DH) + value_bias.reshape(H, DH))).reshape(length, H * DH)
    attn_val = low_back(matmul(context, out_proj) + out_bias)
    hidden = layer_norm(rows + attn_val, attn_gain, attn_shift)
    inner_val = low_back(matmul(low(hidden), inner_proj) + inner_bias)
    active = low(jax.nn.gelu(inner_val, approximate=True))
    outer_val = low_back(matmul(active, outer_proj) + outer_bias)
    return layer_norm(hidden + outer_val, final_gain, final_shift)

def reference(tokens, segment_ids, cotangent, query_proj, key_proj, value_proj, out_proj, value_bias, content_bias, position_bias, position_proj, out_bias, attn_gain, attn_shift, inner_proj, inner_bias, outer_proj, outer_bias, final_gain, final_shift):
    weights = tuple((weight_part.astype(jnp.float32) for weight_part in (query_proj, key_proj, value_proj, out_proj, value_bias, content_bias, position_bias, position_proj, out_bias, attn_gain, attn_shift, inner_proj, inner_bias, outer_proj, outer_bias, final_gain, final_shift)))
    length = tokens.shape[2]
    width = tokens.shape[3]
    all_rows = tokens.astype(jnp.float32).reshape(-1, length, width)
    all_docs = segment_ids.reshape(-1, length)
    all_grads = cotangent.astype(jnp.float32).reshape(-1, length, width)

    def per_sequence(totals, sequence_item):
        rows, doc_ids, grad_rows = sequence_item

        def run(weight_set, inputs):
            return forward(weight_set, inputs, doc_ids)
        result, pull_back = jax.vjp(run, weights, rows)
        weight_grads, input_grad = pull_back(grad_rows)
        totals = jax.tree.map(jnp.add, totals, weight_grads)
        return (totals, (result.astype(jnp.bfloat16), input_grad))
    empty_sums = tuple((jnp.zeros_like(weight_part) for weight_part in weights))
    sums, (outputs, input_grads) = lax.scan(per_sequence, empty_sums, (all_rows, all_docs, all_grads))
    output = outputs.reshape(tokens.shape)
    input_grad = input_grads.reshape(tokens.shape)
    return (output, input_grad, sums[0], sums[1], sums[2], sums[3], sums[4], sums[5], sums[6], sums[7], sums[8], sums[9], sums[10], sums[11], sums[12], sums[13], sums[14], sums[15], sums[16])
```

```python
import math

import jax
import jax.numpy as jnp
from jax import lax
from jax.experimental import pallas as pl
from jax.experimental.pallas import tpu as pltpu
from jax.sharding import Mesh, PartitionSpec as P

H = 16
DH = 64
BLK = 256
NEG = -1e30
BF = jnp.bfloat16
F32 = jnp.float32
ALL = ("dp", "yy", "core")
SEQ = ("yy", "core")
CHIP = ("dp", "yy")


def dot(a, b, ca=1, cb=0):
    return lax.dot_general(a, b, (((ca,), (cb,)), ((), ())), preferred_element_type=F32)


def rotations(length, half_size):
    position = jnp.arange(length, dtype=jnp.int32).astype(F32)
    steps = jnp.arange(half_size, dtype=jnp.int32).astype(F32)
    frequency = jnp.exp(steps * (-math.log(10000.0) / half_size))
    angle = position[:, None] * frequency[None, :]
    return (jnp.cos(angle), jnp.sin(angle))


def layer_norm(values, gain, shift):
    average = jnp.mean(values, axis=-1, keepdims=True)
    centred = values - average
    variance = jnp.mean(centred * centred, axis=-1, keepdims=True)
    return centred * lax.rsqrt(variance + 1e-06) * gain + shift


def gelu_tanh(values):
    return jax.nn.gelu(values, approximate=True)


def swap(x, axis, bit):
    n = lax.axis_size(axis)
    return lax.ppermute(x, axis, [(i, i ^ bit) for i in range(n)])


def side(axis, bit):
    return jnp.where((lax.axis_index(axis) & bit) != 0, 1, 0)


def double(x, axis, bit, dim):
    other = swap(x, axis, bit)
    mine = side(axis, bit) == 0
    return jnp.stack([jnp.where(mine, x, other), jnp.where(mine, other, x)], dim)


def bits_of(axis):
    n = lax.axis_size(axis)
    return [1 << k for k in reversed(range(n.bit_length() - 1))]


def gather_bits(x, axis, dim=0):
    bits = bits_of(axis)
    for k, bit in enumerate(bits):
        x = double(x, axis, bit, dim + k)
    return x.reshape(x.shape[:dim] + (lax.axis_size(axis),) + x.shape[dim + len(bits) :])


def halve(terms, done, order, width):
    left = list(done)
    for axis, bit in order:
        dim = left.index((axis, bit))
        left.pop(dim)
        mine = side(axis, bit)
        send = sum(
            lax.dynamic_index_in_dim(t, 1 - mine, dim, keepdims=False).astype(F32) for t in terms
        ).astype(BF)
        got = swap(send, axis, bit)
        terms = [lax.dynamic_index_in_dim(t, mine, dim, keepdims=False) for t in terms] + [got]
    return sum(t.astype(F32) for t in terms)


def prep_head(e, q, qr, k, kr, first, bias, mat, cos, sin, pk):
    base = jnp.where(first, q, qr) if e == 0 else jnp.where(first, qr, q)
    both = (base + bias).astype(BF)
    turned = dot(both, mat)
    rel = turned[:, :128] * cos + turned[:, 128:] * sin
    qf = (jnp.where(first, both.astype(F32), rel) * (DH**-0.5)).astype(BF)
    kf = jnp.where(first, k if e == 0 else kr, pk).astype(BF)
    return both, qf, kf


def fwd_kernel(
    lohi, q_ref, k_ref, v_ref, segr_ref, segc_ref, cos_ref, sin_ref, pk_ref, bias_ref, mat_ref,
    vb_ref, ctx_ref, o_ref, lse_ref, qf_s, kf_s, sc_s,
):
    m = pl.program_id(0)
    nb = q_ref.shape[1] // BLK
    first = lax.broadcasted_iota(jnp.int32, (BLK, 128), 1) < DH

    def prep(i, c):
        rows = pl.ds(pl.multiple_of(i * BLK, BLK), BLK)
        q = q_ref[0, rows, :].astype(F32)
        k = k_ref[0, rows, :].astype(F32)
        qr, kr = pltpu.roll(q, DH, 1), pltpu.roll(k, DH, 1)
        for e in range(2):
            _, qf, kf = prep_head(
                e, q, qr, k, kr, first, bias_ref[0, e : e + 1, :], mat_ref[0, e],
                cos_ref[rows, :], sin_ref[rows, :], pk_ref[rows, :],
            )
            qf_s[e, rows, :] = qf
            kf_s[e, rows, :] = kf
        return c

    lax.fori_loop(0, nb, prep, 0)

    def q_block(i, c):
        rows = pl.ds(pl.multiple_of(i * BLK, BLK), BLK)
        at = (m * nb + i) * 2
        lo, hi = lohi[at], lohi[at + 1]
        segq = segc_ref[0, rows, :]
        segq = jnp.concatenate([segq] * (BLK // 128), 1)
        outs = []
        for e in range(2):
            qf = qf_s[e, rows, :]

            def scores(j, top, e=e, qf=qf):
                cols = pl.ds(pl.multiple_of(j * BLK, BLK), BLK)
                s = dot(qf, kf_s[e, cols, :], 1, 1)
                s = jnp.where(segq == segr_ref[0, j], s, NEG)
                sc_s[j] = s
                for g in range(BLK // 128):
                    top = jnp.maximum(top, s[:, g * 128 : g * 128 + 128])
                return top

            top = lax.fori_loop(lo, hi, scores, jnp.full((BLK, 128), NEG, F32))
            top = jnp.max(top, axis=1, keepdims=True)

            def mix(j, carry):
                total, acc = carry
                cols = pl.ds(pl.multiple_of(j * BLK, BLK), BLK)
                p = jnp.exp(sc_s[j] - top)
                for g in range(BLK // 128):
                    total = total + p[:, g * 128 : g * 128 + 128]
                acc = acc + dot(p.astype(BF), v_ref[0, cols, :])
                return total, acc

            zero = jnp.zeros((BLK, 128), F32)
            total, acc = lax.fori_loop(lo, hi, mix, (zero, zero))
            total = jnp.sum(total, axis=1, keepdims=True)
            outs.append((acc / total, top + jnp.log(total)))
        o = jnp.where(first, outs[0][0], outs[1][0])
        o_ref[0, rows, :] = o
        lse_ref[0, rows, :] = jnp.where(first, outs[0][1], outs[1][1])
        ctx_ref[0, rows, :] = (o + vb_ref[0]).astype(BF)
        return c

    lax.fori_loop(0, nb, q_block, 0)


def bwd_kernel(
    lohi, q_ref, k_ref, v_ref, g_ref, o_ref, lse_ref, segr_ref, segc_ref, cos_ref, sin_ref,
    pk_ref, bias_ref, mat_ref, matt_ref, gqkv_ref, gsm_ref, gpp_ref,
    both_s, qf_s, kf_s, lse_s, dl_s, gq_s, res_s,
):
    m, p = pl.program_id(0), pl.program_id(1)
    nb = q_ref.shape[1] // BLK
    width = gqkv_ref.shape[2] // 3
    first = lax.broadcasted_iota(jnp.int32, (BLK, 128), 1) < DH

    def prep(i, c):
        rows = pl.ds(pl.multiple_of(i * BLK, BLK), BLK)
        q = q_ref[0, rows, :].astype(F32)
        k = k_ref[0, rows, :].astype(F32)
        qr, kr = pltpu.roll(q, DH, 1), pltpu.roll(k, DH, 1)
        lse_t = lse_ref[0, rows, :].T
        dl_t = (g_ref[0, rows, :].astype(F32) * o_ref[0, rows, :]).T
        for e in range(2):
            both, qf, kf = prep_head(
                e, q, qr, k, kr, first, bias_ref[0, e : e + 1, :], mat_ref[0, e],
                cos_ref[rows, :], sin_ref[rows, :], pk_ref[rows, :],
            )
            both_s[e, rows, :] = both
            qf_s[e, rows, :] = qf
            kf_s[e, rows, :] = kf
            lse_s[e, i] = lse_t[e * DH : e * DH + 8, :]
            dl = jnp.sum(dl_t[e * DH : (e + 1) * DH, :], axis=0, keepdims=True)
            dl_s[e, i] = jnp.broadcast_to(dl, (8, BLK))
        return c

    lax.fori_loop(0, nb, prep, 0)

    for e in range(2):
        mine = first if e == 0 else jnp.logical_not(first)

        def clear(i, c):
            gq_s[pl.ds(pl.multiple_of(i * BLK, BLK), BLK), :] = jnp.zeros((BLK, 128), F32)
            return c

        lax.fori_loop(0, nb, clear, 0)

        def k_block(j, c, e=e, mine=mine):
            rows = pl.ds(pl.multiple_of(j * BLK, BLK), BLK)
            at = (m * nb + j) * 2
            lo, hi = lohi[at], lohi[at + 1]
            kf = kf_s[e, rows, :]
            vm = jnp.where(mine, v_ref[0, rows, :].astype(F32), 0.0).astype(BF)
            segk = jnp.concatenate([segc_ref[0, rows, :]] * (BLK // 128), 1)

            def q_step(i, carry):
                gk, gv = carry
                cols = pl.ds(pl.multiple_of(i * BLK, BLK), BLK)
                qf = qf_s[e, cols, :]
                g = g_ref[0, cols, :]
                s = dot(kf, qf, 1, 1) - lse_s[e, i, 0:1, :]
                prob = jnp.where(segk == segr_ref[0, i], jnp.exp(s), 0.0)
                gp = dot(vm, g, 1, 1) - dl_s[e, i, 0:1, :]
                ds = (prob * gp).astype(BF)
                gv = gv + dot(prob.astype(BF), g)
                gk = gk + dot(ds, qf)
                gq_s[cols, :] = gq_s[cols, :] + dot(ds, kf, 0, 0)
                return gk, gv

            zero = jnp.zeros((BLK, 128), F32)
            gk, gv = lax.fori_loop(lo, hi, q_step, (zero, zero))
            if e == 0:
                res_s[1, rows, :] = gk
                res_s[2, rows, :] = gv
            else:
                res_s[1, rows, :] = jnp.where(first, res_s[1, rows, :], pltpu.roll(gk, DH, 1))
                res_s[2, rows, :] = jnp.where(first, res_s[2, rows, :], gv)
            return c

        lax.fori_loop(0, nb, k_block, 0)

        def finish(i, carry, e=e):
            s_content, s_pos, s_proj = carry
            rows = pl.ds(pl.multiple_of(i * BLK, BLK), BLK)
            g = gq_s[rows, :] * (DH**-0.5)
            turned = jnp.concatenate(
                [(g * cos_ref[rows, :]).astype(BF), (g * sin_ref[rows, :]).astype(BF)], 1
            )
            gqp = dot(turned, matt_ref[0, e])
            gq = g + gqp
            if e == 0:
                res_s[0, rows, :] = gq
            else:
                res_s[0, rows, :] = jnp.where(first, res_s[0, rows, :], pltpu.roll(gq, DH, 1))
            s_content = s_content + jnp.sum(g, axis=0, keepdims=True)
            s_pos = s_pos + jnp.sum(gqp, axis=0, keepdims=True)
            s_proj = s_proj + dot(both_s[e, rows, :], turned, 0, 0)
            return s_content, s_pos, s_proj

        row = jnp.zeros((1, 128), F32)
        s_content, s_pos, s_proj = lax.fori_loop(
            0, nb, finish, (row, row, jnp.zeros((128, 256), F32))
        )
        gsm_ref[0, 0, e, 0:1, :] = s_content
        gsm_ref[0, 0, e, 1:2, :] = s_pos
        gpp_ref[0, 0, e] = s_proj

    for at in range(width // 128):

        @pl.when(p == at)
        def _(at=at):
            for part in range(3):
                off = part * width + at * 128
                gqkv_ref[0, :, off : off + 128] = res_s[part].astype(BF)


def attention_specs(L, width):
    pairs = width // 128
    pair = lambda k: pl.BlockSpec((1, L, 128), lambda m, p, *_: (m, 0, k * pairs + p))
    per_m = lambda *s: pl.BlockSpec((1,) + s, lambda m, p, *_: (m,) + (0,) * len(s))
    per_p = lambda *s: pl.BlockSpec((1,) + s, lambda m, p, *_: (p,) + (0,) * len(s))
    whole = lambda *s: pl.BlockSpec(s, lambda m, p, *_: (0,) * len(s))
    return pairs, pair, per_m, per_p, whole


def attention_forward(qkv, lohi, segr, segc, cos, sin, pk, bias, mat, vb):
    M, L, w3 = qkv.shape
    width = w3 // 3
    nb = L // BLK
    pairs, pair, per_m, per_p, whole = attention_specs(L, width)
    return pl.pallas_call(
        fwd_kernel,
        out_shape=(
            jax.ShapeDtypeStruct((M, L, width), BF),
            jax.ShapeDtypeStruct((M, L, width), F32),
            jax.ShapeDtypeStruct((M, L, width), F32),
        ),
        grid_spec=pltpu.PrefetchScalarGridSpec(
            num_scalar_prefetch=1,
            grid=(M, pairs),
            in_specs=[
                pair(0), pair(1), pair(2), per_m(nb, 1, BLK), per_m(L, 128), whole(L, 128),
                whole(L, 128), whole(L, 128), per_p(2, 128), per_p(2, 128, 256), per_p(1, 128),
            ],
            out_specs=[pair(0), pair(0), pair(0)],
            scratch_shapes=[
                pltpu.VMEM((2, L, 128), BF),
                pltpu.VMEM((2, L, 128), BF),
                pltpu.VMEM((nb, BLK, BLK), F32),
            ],
        ),
        compiler_params=pltpu.CompilerParams(
            dimension_semantics=("arbitrary", "arbitrary"), vmem_limit_bytes=32 << 20
        ),
        name="attend",
    )(lohi, qkv, qkv, qkv, segr, segc, cos, sin, pk, bias, mat, vb)


def attention_backward(qkv, g, o, lse, lohi, segr, segc, cos, sin, pk, bias, mat, matt):
    M, L, w3 = qkv.shape
    width = w3 // 3
    nb = L // BLK
    pairs, pair, per_m, per_p, whole = attention_specs(L, width)
    per_mp = lambda *s: pl.BlockSpec((1, 1) + s, lambda m, p, *_: (m, p) + (0,) * len(s))
    return pl.pallas_call(
        bwd_kernel,
        out_shape=(
            jax.ShapeDtypeStruct((M, L, w3), BF),
            jax.ShapeDtypeStruct((M, pairs, 2, 8, 128), F32),
            jax.ShapeDtypeStruct((M, pairs, 2, 128, 256), F32),
        ),
        grid_spec=pltpu.PrefetchScalarGridSpec(
            num_scalar_prefetch=1,
            grid=(M, pairs),
            in_specs=[
                pair(0), pair(1), pair(2), pair(0), pair(0), pair(0), per_m(nb, 1, BLK),
                per_m(L, 128), whole(L, 128), whole(L, 128), whole(L, 128), per_p(2, 128),
                per_p(2, 128, 256), per_p(2, 256, 128),
            ],
            out_specs=[per_m(L, w3), per_mp(2, 8, 128), per_mp(2, 128, 256)],
            scratch_shapes=[
                pltpu.VMEM((2, L, 128), BF),
                pltpu.VMEM((2, L, 128), BF),
                pltpu.VMEM((2, L, 128), BF),
                pltpu.VMEM((2, nb, 8, BLK), F32),
                pltpu.VMEM((2, nb, 8, BLK), F32),
                pltpu.VMEM((L, 128), F32),
                pltpu.VMEM((3, L, 128), F32),
            ],
        ),
        compiler_params=pltpu.CompilerParams(
            dimension_semantics=("arbitrary", "arbitrary"), vmem_limit_bytes=40 << 20
        ),
        name="attend_back",
    )(lohi, qkv, qkv, qkv, g, o, lse, segr, segc, cos, sin, pk, bias, mat, matt)


def per_device(
    tokens, segment_ids, cotangent, query_proj, key_proj, value_proj, out_proj, value_bias,
    content_bias, position_bias, position_proj, out_bias, attn_gain, attn_shift, inner_proj,
    inner_bias, outer_proj, outer_bias, final_gain, final_shift,
):
    M, _, T, D = tokens.shape
    n_dp, n_yy, n_core = (lax.axis_size(a) for a in ALL)
    S = n_yy * n_core
    chips = n_dp * n_yy
    devices = chips * n_core
    L = T * S
    R = query_proj.shape[0]
    U = outer_proj.shape[0]
    FF = U * devices
    hl = H // S
    width = hl * DH
    pairs = width // 128
    half = DH // 2
    N = M * T
    core = lax.axis_index("core")
    seq = lax.axis_index("yy") * n_core + core
    dp_bits = [("dp", b) for b in bits_of("dp")]
    yy_bits = [("yy", b) for b in bits_of("yy")]
    two = lambda bits: (2,) * len(bits)

    smalls = [
        content_bias, position_bias, position_proj.reshape(-1), value_bias, out_bias, attn_gain,
        attn_shift, outer_bias, final_gain, final_shift, inner_bias,
    ]
    sizes = [s.size for s in smalls]
    w3 = 3 * width
    extra = -(-sum(sizes) // w3)
    packed = jnp.concatenate(smalls + [jnp.zeros((extra * w3 - sum(sizes),), BF)])
    packed = jnp.broadcast_to(packed.reshape(1, extra, w3), (S, extra, w3))
    by_seq = jnp.stack([query_proj, key_proj, value_proj], 0).reshape(3, R, S, width)
    by_seq = by_seq.transpose(2, 1, 0, 3).reshape(S, R, w3)
    mixed = lax.all_to_all(
        jnp.concatenate([by_seq, packed], 1), SEQ, split_axis=0, concat_axis=0, tiled=True
    )
    mixed = gather_bits(mixed, "dp")
    w_qkv = mixed[:, :, :R].reshape(D, w3)
    flat = mixed[:, :, R:].reshape(devices, extra * w3)
    full, at = [], 0
    for size in sizes:
        full.append(flat[:, at : at + size])
        at += size
    heads = lambda v: lax.dynamic_slice_in_dim(v.reshape(S, -1), seq, 1, 0)
    full_content, full_posbias, full_posproj, full_vbias = full[:4]
    vec = lambda v: v.reshape(1, -1).astype(F32)
    full_obias, full_again, full_ashift, full_fbias, full_fgain, full_fshift = map(vec, full[4:10])
    ib = lax.dynamic_index_in_dim(full[10].reshape(chips, n_core, 2, U // 2), core, 1, False)
    full_ibias = ib.transpose(1, 0, 2).reshape(1, -1).astype(F32)

    inner_cols = inner_proj.reshape(R, chips, n_core, 2, U // 2).transpose(2, 0, 3, 1, 4)
    inner_cols = inner_cols.reshape(n_core, R, FF // n_core)
    inner_mine = lax.all_to_all(inner_cols, "core", split_axis=0, concat_axis=0, tiled=True)
    inner_mine = inner_mine.reshape(n_core * R, FF // n_core)
    out_mine = lax.all_gather(out_proj, "core", axis=0, tiled=True)
    outer_mine = jnp.concatenate([outer_proj[: U // 2], outer_proj[U // 2 :]], 1)
    big = jnp.concatenate([inner_mine, out_mine, outer_mine], 1)
    big = lax.all_gather(big, CHIP, axis=0, tiled=True)
    FH = FF // n_core
    w_inner = big[:, :FH]
    w_out = big[:, FH : FH + D]
    w_outer = [big[:, FH + D + k * D : FH + 2 * D + k * D] for k in range(2)]

    x = tokens[:, 0]
    x_all = x
    for k, (axis, bit) in enumerate(yy_bits):
        x_all = double(x_all, axis, bit, 1 + k)
    x_all = x_all.reshape(M, n_yy, T, D)
    x_all = double(x_all, "core", 1, 2).reshape(M * L, D)
    docs = lax.all_gather(segment_ids[:, 0], SEQ, axis=1, tiled=True)
    nb = L // BLK
    ends = docs.reshape(M, nb, BLK)
    lo = jnp.sum(docs[:, None, :] < ends[:, :, :1], -1) // BLK
    hi = (jnp.sum(docs[:, None, :] <= ends[:, :, -1:], -1) + BLK - 1) // BLK
    lohi = jnp.stack([lo, hi], -1).reshape(-1).astype(jnp.int32)
    segr = docs.reshape(M, nb, 1, BLK)
    segc = jnp.broadcast_to(docs[:, :, None], (M, L, 128))
    cos_t, sin_t = rotations(L, half)
    none = jnp.zeros((L, DH), F32)
    cos2 = jnp.concatenate([none, cos_t, cos_t], 1)
    sin2 = jnp.concatenate([none, sin_t, sin_t], 1)
    pk2 = jnp.concatenate([none, cos_t, sin_t], 1).astype(BF).astype(F32)
    bias = jnp.stack(
        [heads(full_content).reshape(hl, DH), heads(full_posbias).reshape(hl, DH)], 1
    )
    bias = bias.reshape(pairs, 2, 2 * DH).astype(F32)
    pp = heads(full_posproj).reshape(hl, DH, DH)
    pc, ps = pp[..., :half], pp[..., half:]
    z64 = jnp.zeros((hl, DH, DH), BF)
    mat = jnp.concatenate([z64, pc, -ps, z64, ps, pc], 2)
    mat = jnp.concatenate([jnp.zeros_like(mat), mat], 1).reshape(pairs, 2, 128, 256)
    matt = jnp.swapaxes(mat[:, :, DH:, :], 2, 3)
    matt = jnp.concatenate([matt, jnp.zeros_like(matt)], 3)
    vb = heads(full_vbias).reshape(pairs, 1, 128).astype(F32)

    qkv = dot(x_all, w_qkv).astype(BF).reshape(M, L, w3)
    ctx, o, lse = attention_forward(qkv, lohi, segr, segc, cos2, sin2, pk2, bias, mat, vb)
    ctx_tok = lax.all_to_all(
        ctx.reshape(M, S, T, width), SEQ, split_axis=1, concat_axis=1, tiled=True
    )
    ctx_tok = ctx_tok.transpose(0, 2, 1, 3).reshape(N, H * DH)
    x_float = x.reshape(N, D).astype(F32)
    attn = dot(ctx_tok, w_out) + full_obias
    hidden, first_back = jax.vjp(
        lambda a, g, b: layer_norm(a, g, b), x_float + attn, full_again, full_ashift
    )
    pair = lambda v: jnp.concatenate([v, swap(v, "core", 1)], 0)
    hid_pair = pair(hidden.astype(BF))
    inner = dot(hid_pair, w_inner) + full_ibias
    active, gelu_back = jax.vjp(gelu_tanh, inner)
    active = active.astype(BF)
    part = dot(active[:, :D], w_outer[0]) if FH == D else None
    FQ = FH // 2
    part = dot(active[:, :FQ], w_outer[0]) + dot(active[:, FQ:], w_outer[1])
    outer = part[:N] + swap(part[N:].astype(BF), "core", 1).astype(F32) + full_fbias
    result, second_back = jax.vjp(
        lambda a, g, b: layer_norm(a, g, b), hidden + outer, full_fgain, full_fshift
    )
    output = result.astype(BF).reshape(M, 1, T, D)

    g_hidden, g_fgain, g_fshift = second_back(cotangent[:, 0].reshape(N, D).astype(F32))
    go = g_hidden.astype(BF)
    go_pair = pair(go)
    g_outer_w = [dot(active[:, k * FQ : (k + 1) * FQ], go_pair, 0, 0).astype(BF) for k in range(2)]
    g_active = jnp.concatenate([dot(go_pair, w, 1, 1) for w in w_outer], 1)
    (g_inner,) = gelu_back(g_active)
    gi = g_inner.astype(BF)
    g_part = dot(gi, w_inner, 1, 1)
    g_inner_w = dot(hid_pair, gi, 0, 0).astype(BF)
    g_hidden = g_hidden + g_part[:N] + swap(g_part[N:].astype(BF), "core", 1).astype(F32)
    g_sum, g_again, g_ashift = first_back(g_hidden)
    ga = g_sum.astype(BF)
    gc = dot(ga, w_out, 1, 1).astype(BF)
    g_heads = lax.all_to_all(
        gc.reshape(M, T, S, width).transpose(0, 2, 1, 3), SEQ, split_axis=1, concat_axis=1, tiled=True
    ).reshape(M, L, width)
    g_out_w = dot(ctx_tok, ga, 0, 0).astype(BF)
    gqkv, gsm, gpp = attention_backward(
        qkv, g_heads, o, lse, lohi, segr, segc, cos2, sin2, pk2, bias, mat, matt
    )
    gqkv = gqkv.reshape(M * L, w3)

    dx = dot(gqkv, w_qkv, 1, 1).astype(BF)
    dx = halve(
        [dx.reshape((M,) + two(yy_bits) + (2, T, D)).transpose(
            tuple(range(1, len(yy_bits) + 2)) + (0, len(yy_bits) + 2, len(yy_bits) + 3)
        )],
        yy_bits + [("core", 1)],
        [("core", 1)] + yy_bits,
        D,
    )
    input_grad = (g_sum + dx.reshape(N, D)).reshape(M, 1, T, D)

    g_qkv_w = dot(x_all, gqkv, 0, 0).astype(BF)
    colsum = lambda v: jnp.sum(v.astype(F32), axis=0)
    spread = lambda v: lax.dynamic_update_slice(
        jnp.zeros((S, v.size), F32), v.reshape(1, -1), (seq, 0)
    ).reshape(devices, -1)
    gsm = jnp.sum(gsm, 0)[:, :, :2, :DH].reshape(hl, 2, DH)
    gpp = jnp.sum(gpp, 0).reshape(hl, 128, 256)[:, DH:]
    e1, e2 = gpp[:, :, DH : 2 * DH], gpp[:, :, 3 * DH :]
    g_posproj = jnp.concatenate(
        [e1[..., :half] + e2[..., half:], e2[..., :half] - e1[..., half:]], -1
    )
    own = lambda v: v.reshape(devices, -1)
    g_ibias = colsum(gi).reshape(2, chips, 1, U // 2).transpose(1, 2, 0, 3).reshape(chips, 1, U)
    on_core = (jnp.arange(n_core) == core).reshape(1, n_core, 1)
    g_ibias = jnp.where(on_core, g_ibias, 0.0).reshape(devices, U)
    g_smalls = jnp.concatenate(
        [
            spread(gsm[:, 0]), spread(gsm[:, 1]), spread(g_posproj), own(colsum(gc)),
            own(colsum(ga)), own(g_again), own(g_ashift), own(colsum(go)), own(g_fgain),
            own(g_fshift), g_ibias, jnp.zeros((devices, extra * w3 - sum(sizes)), F32),
        ],
        1,
    )
    g_smalls = g_smalls.astype(BF).reshape(two(dp_bits + yy_bits) + (2, extra, w3))
    g_smalls = halve(
        [g_smalls], dp_bits + yy_bits + [("core", 1)], [("core", 1)] + yy_bits, w3
    ).astype(BF)
    g_mixed = jnp.concatenate(
        [g_qkv_w.reshape(two(dp_bits) + (S * R, w3)), g_smalls], len(dp_bits)
    )
    g_mixed = halve([g_mixed], dp_bits, dp_bits[::-1], w3)
    g_small = g_mixed[S * R :].reshape(-1)
    g_rows = lax.all_to_all(
        g_mixed[: S * R].astype(BF).reshape(S, R, 3, width), SEQ, split_axis=0, concat_axis=0,
        tiled=True,
    )
    g_rows = g_rows.astype(F32).transpose(2, 1, 0, 3).reshape(3, R, D)
    small_grads, at = [], 0
    for size, like in zip(sizes, smalls):
        small_grads.append(g_small[at : at + size])
        at += size

    chip_bits = dp_bits + yy_bits
    orders = [yy_bits + dp_bits[::-1], dp_bits[::-1][:1] + yy_bits + dp_bits[::-1][1:]]
    rows = two(chip_bits) + (n_core * R,)
    red_outer = [
        halve([g.reshape(rows + (D,))], chip_bits, orders[k], D) for k, g in enumerate(g_outer_w)
    ]
    red_inner = [
        halve([g_inner_w[:, k * FQ : (k + 1) * FQ].reshape(rows + (FQ,))], chip_bits, orders[k], FQ)
        for k in range(2)
    ]
    go2 = g_out_w.reshape(D, n_core, D // n_core)
    mine = lax.dynamic_index_in_dim(go2, core, 1, False).astype(F32)
    theirs = lax.dynamic_index_in_dim(go2, 1 - core, 1, False)
    g_out_half = (mine + swap(theirs, "core", 1).astype(F32)).astype(BF)
    red_out = halve([g_out_half.reshape(rows + (D // n_core,))], chip_bits, orders[0], D)
    red_inner = jnp.concatenate(red_inner, 1).astype(BF).reshape(n_core, R, FH)
    red_inner = lax.all_to_all(red_inner, "core", split_axis=0, concat_axis=0, tiled=True)
    inner_grad = red_inner.reshape(n_core, R, 2, chips, U // 2).transpose(1, 3, 0, 2, 4)
    inner_grad = inner_grad.astype(F32).reshape(R, FF)
    red_out = lax.all_to_all(
        red_out.astype(BF).reshape(n_core, R, D // n_core), "core", split_axis=0, concat_axis=0,
        tiled=True,
    )
    out_grad = red_out.astype(F32).transpose(1, 0, 2).reshape(R, D)
    outer_grad = jnp.concatenate(red_outer, 0)

    s = small_grads
    return (
        output, input_grad, g_rows[0], g_rows[1], g_rows[2], out_grad, s[3], s[0], s[1],
        s[2].reshape(R, DH), s[4], s[5], s[6], inner_grad, s[10], outer_grad, s[7], s[8], s[9],
    )


def solution(mesh):
    n_dp, n_seq = mesh.devices.shape
    mesh = Mesh(mesh.devices.reshape(n_dp, n_seq // 2, 2), ALL)
    tok, ids = P(None, "dp", SEQ, None), P(None, "dp", SEQ)
    mat, vec = P(ALL, None), P(ALL)
    in_specs = (
        tok, ids, tok, mat, mat, mat, mat, vec, vec, vec, mat, vec, vec, vec, mat, vec, mat, vec,
        vec, vec,
    )
    out_specs = (
        tok, tok, mat, mat, mat, mat, vec, vec, vec, mat, vec, vec, vec, mat, vec, mat, vec, vec,
        vec,
    )
    return jax.shard_map(
        per_device, mesh=mesh, in_specs=in_specs, out_specs=out_specs, check_vma=False
    )
```

```python
import functools
import math

import jax
import jax.numpy as jnp
from jax import lax
from jax.experimental import pallas as pl
from jax.experimental.pallas import tpu as pltpu
from jax.sharding import Mesh, PartitionSpec as P

H = 16
DH = 64
BLK = 256
GRP = 2
NEG = -1e30
BF = jnp.bfloat16
F32 = jnp.float32
DP = ("dz", "dx")
SEQ = ("yy", "core")
CHIP = DP + ("yy",)
ALL = DP + SEQ


def dot(a, b, ca=1, cb=0):
    return lax.dot_general(a, b, (((ca,), (cb,)), ((), ())), preferred_element_type=F32)


def rotations(length, half_size):
    position = jnp.arange(length, dtype=jnp.int32).astype(F32)
    steps = jnp.arange(half_size, dtype=jnp.int32).astype(F32)
    frequency = jnp.exp(steps * (-math.log(10000.0) / half_size))
    angle = position[:, None] * frequency[None, :]
    return (jnp.cos(angle), jnp.sin(angle))


def layer_norm(values, gain, shift):
    average = jnp.mean(values, axis=-1, keepdims=True)
    centred = values - average
    variance = jnp.mean(centred * centred, axis=-1, keepdims=True)
    return centred * lax.rsqrt(variance + 1e-06) * gain + shift


def gelu_tanh(values):
    return jax.nn.gelu(values, approximate=True)


def swap(x, axis, bit):
    n = lax.axis_size(axis)
    return lax.ppermute(x, axis, [(i, i ^ bit) for i in range(n)])


def side(axis, bit):
    return jnp.where((lax.axis_index(axis) & bit) != 0, 1, 0)


def double(x, axis, bit, dim, other=None):
    other = swap(x, axis, bit) if other is None else other
    mine = side(axis, bit) == 0
    return jnp.stack([jnp.where(mine, x, other), jnp.where(mine, other, x)], dim)


def bits_of(axis):
    n = lax.axis_size(axis)
    return [1 << k for k in reversed(range(n.bit_length() - 1))]


def gather_bits(x, axis, dim=0, wait=None):
    bits = bits_of(axis)
    for k, bit in enumerate(bits):
        x = double(x, axis, bit, dim + k)
        if wait is not None and k == 0:
            behind = tuple(wait)
            wait.append(x)
            x = after(x, *behind)
    return x.reshape(x.shape[:dim] + (lax.axis_size(axis),) + x.shape[dim + len(bits) :])


def total(terms):
    return sum(t.astype(F32) for t in terms)


class Chain:
    def __init__(self, terms, left):
        self.terms, self.left, self.sends = terms, list(left), []

    def send(self, step):
        axis, bit = step
        dim = self.left.index(step)
        self.left.pop(dim)
        mine = side(axis, bit)
        take = lambda t, k: lax.dynamic_index_in_dim(t, k, dim, keepdims=False)
        out = total([take(t, 1 - mine) for t in self.terms]).astype(BF)
        self.terms = [take(t, mine) for t in self.terms]
        self.sends.append(out)
        return out

    def run(self, steps):
        for step in steps:
            got = swap(self.send(step), *step)
            self.terms.append(got)
        return self

    def result(self):
        return total(self.terms)


def run_together(chains, steps):
    sends = []
    for step in steps:
        parts = [c.send(step) for c in chains]
        sends.append(jnp.concatenate(parts, -1))
        got, at = swap(sends[-1], *step), 0
        for c, part in zip(chains, parts):
            c.terms.append(got[..., at : at + part.shape[-1]])
            at += part.shape[-1]
    return sends


def after(x, *others):
    return lax.optimization_barrier((x,) + others)[0]


def meet(x, *chains):
    x, last = lax.optimization_barrier((x, [c.terms[-1] for c in chains]))
    for c, t in zip(chains, last):
        c.terms[-1] = t
    return x


def tables(tab):
    lane = lax.broadcasted_iota(jnp.int32, tab.shape, 1)
    turned = pltpu.roll(tab, DH, 1)
    cos = jnp.where(lane < DH, 0.0, tab)
    sin = jnp.where(lane < DH, 0.0, turned)
    return cos, sin, jnp.where(lane < DH + DH // 2, tab, turned)


def prep_head(e, q, qr, k, kr, first, bias, mat, cos, sin, pk):
    base = jnp.where(first, q, qr) if e == 0 else jnp.where(first, qr, q)
    both = (base + bias).astype(BF)
    turned = dot(both, mat)
    rel = turned[:, :128] * cos + turned[:, 128:] * sin
    qf = (jnp.where(first, both.astype(F32), rel) * (DH**-0.5)).astype(BF)
    kf = jnp.where(first, k if e == 0 else kr, pk).astype(BF)
    return both, qf, kf


def row_of(ref, start, width):
    return jnp.concatenate([ref[0, start + t] for t in range(width // 128)], 1)


def seg_columns(segr_ref, seg_s, i):
    for t in range(i * (BLK // 128), (i + 1) * (BLK // 128)):
        tile = jnp.broadcast_to(segr_ref[0, t], (128, 128)).T
        seg_s[t * 128 : (t + 1) * 128, :] = tile


def by_width(n, most, body):
    for k in range(1, most + 1):

        @pl.when(n == k)
        def _(k=k):
            body(k * BLK)


def fwd_kernel(
    lohi, q_ref, k_ref, v_ref, segr_ref, tab_ref, bias_ref, mat_ref, vb_ref,
    ctx_ref, o_ref, lse_ref, qf_s, kf_s, seg_s,
):
    m = pl.program_id(0)
    nb = q_ref.shape[1] // BLK
    first = lax.broadcasted_iota(jnp.int32, (BLK, 128), 1) < DH

    def prep(i):
        rows = slice(i * BLK, (i + 1) * BLK)
        seg_columns(segr_ref, seg_s, i)
        q = q_ref[0, rows, :].astype(F32)
        k = k_ref[0, rows, :].astype(F32)
        qr, kr = pltpu.roll(q, DH, 1), pltpu.roll(k, DH, 1)
        cos, sin, pk = tables(tab_ref[rows, :])
        for e in range(2):
            _, qf, kf = prep_head(
                e, q, qr, k, kr, first, bias_ref[0, e : e + 1, :], mat_ref[0, e],
                cos, sin, pk,
            )
            qf_s[e, rows, :] = qf
            kf_s[e, rows, :] = kf

    for i in range(nb):
        prep(i)

    def q_group(i, c):
        at = (m * nb + i * GRP) * 2
        starts = [lohi[at + 2 * u] for u in range(GRP)]
        n = lohi[at + 1]
        for u in range(1, GRP):
            n = jnp.maximum(n, lohi[at + 2 * u + 1])

        def body(width):
            for u in range(GRP):
                rows = pl.ds(pl.multiple_of((i * GRP + u) * BLK, BLK), BLK)
                start = jnp.minimum(starts[u], (nb * BLK - width) // 128)
                cols = pl.ds(pl.multiple_of(start * 128, 128), width)
                segq = jnp.concatenate([seg_s[rows, :]] * (width // 128), 1)
                same = segq == row_of(segr_ref, start, width)
                outs = []
                for e in range(2):
                    s = dot(qf_s[e, rows, :], kf_s[e, cols, :], 1, 1)
                    s = jnp.where(same, s, NEG)
                    top = jnp.max(s, axis=1, keepdims=True)
                    p = jnp.exp(s - top)
                    total = jnp.sum(p, axis=1, keepdims=True)
                    acc = dot(p.astype(BF), v_ref[0, cols, :])
                    outs.append((acc / total, top + jnp.log(total)))
                o = jnp.where(first, outs[0][0], outs[1][0])
                o_ref[0, rows, :] = o.astype(BF)
                lse_t = jnp.where(first, outs[0][1], outs[1][1]).T
                for e in range(2):
                    for t in range(BLK // 128):
                        lse_ref[0, 0, e, (i * GRP + u) * (BLK // 128) + t] = lse_t[
                            e * DH : e * DH + 1, t * 128 : t * 128 + 128
                        ]
                ctx_ref[0, rows, :] = (o + vb_ref[0]).astype(BF)

        by_width(n, nb, body)
        return c

    lax.fori_loop(0, nb // GRP, q_group, 0)


def bwd_kernel(
    m, lohi, q_ref, k_ref, v_ref, g_ref, o_ref, lse_ref, segr_ref, tab_ref, bias_ref,
    mat_ref, *refs,
):
    gqkv_ref, gsm_ref, gpp_ref, both_s, qf_s, kf_s, seg_s, dl_s, gq_s, res_s = refs[-10:]
    p = pl.program_id(0)
    nb = q_ref.shape[1] // BLK
    width3 = gqkv_ref.shape[2] // 3
    first = lax.broadcasted_iota(jnp.int32, (BLK, 128), 1) < DH

    def prep(i):
        rows = slice(i * BLK, (i + 1) * BLK)
        seg_columns(segr_ref, seg_s, i)
        q = q_ref[0, rows, :].astype(F32)
        k = k_ref[0, rows, :].astype(F32)
        qr, kr = pltpu.roll(q, DH, 1), pltpu.roll(k, DH, 1)
        cos, sin, pk = tables(tab_ref[rows, :])
        dl_t = (g_ref[0, rows, :].astype(F32) * o_ref[0, rows, :].astype(F32)).T
        for e in range(2):
            both, qf, kf = prep_head(
                e, q, qr, k, kr, first, bias_ref[0, e : e + 1, :], mat_ref[0, e],
                cos, sin, pk,
            )
            both_s[e, rows, :] = both
            qf_s[e, rows, :] = qf
            kf_s[e, rows, :] = kf
            gq_s[e, rows, :] = jnp.zeros((BLK, 128), F32)
            dl = jnp.sum(dl_t[e * DH : (e + 1) * DH, :], axis=0, keepdims=True)
            for t in range(BLK // 128):
                dl_s[e, i * (BLK // 128) + t] = dl[:, t * 128 : t * 128 + 128]

    for i in range(nb):
        prep(i)

    def k_group(j, c):
        at = (m * nb + j * GRP) * 2
        starts = [lohi[at + 2 * u] for u in range(GRP)]
        n = lohi[at + 1]
        for u in range(1, GRP):
            n = jnp.maximum(n, lohi[at + 2 * u + 1])

        def body(width):
            for u in range(GRP):
                rows = pl.ds(pl.multiple_of((j * GRP + u) * BLK, BLK), BLK)
                start = jnp.minimum(starts[u], (nb * BLK - width) // 128)
                cols = pl.ds(pl.multiple_of(start * 128, 128), width)
                segk = jnp.concatenate([seg_s[rows, :]] * (width // 128), 1)
                same = segk == row_of(segr_ref, start, width)
                g = g_ref[0, cols, :]
                v = v_ref[0, rows, :].astype(F32)
                outs = []
                for e in range(2):
                    row = lambda ref: jnp.concatenate(
                        [ref[e, start + t] for t in range(width // 128)], 1
                    )
                    mine = first if e == 0 else jnp.logical_not(first)
                    vm = jnp.where(mine, v, 0.0).astype(BF)
                    kf, qf = kf_s[e, rows, :], qf_s[e, cols, :]
                    prob = jnp.where(same, jnp.exp(dot(kf, qf, 1, 1) - row(lse_ref.at[0, 0])), 0.0)
                    ds = (prob * (dot(vm, g, 1, 1) - row(dl_s))).astype(BF)
                    gv = dot(prob.astype(BF), g)
                    gk = dot(ds, qf)
                    gq_s[e, cols, :] = gq_s[e, cols, :] + dot(ds, kf, 0, 0)
                    outs.append((gk, gv))
                res_s[1, rows, :] = jnp.where(first, outs[0][0], pltpu.roll(outs[1][0], DH, 1))
                res_s[2, rows, :] = jnp.where(first, outs[0][1], outs[1][1])

        by_width(n, nb, body)
        return c

    lax.fori_loop(0, nb // GRP, k_group, 0)

    def finish(i, carry):
        rows = pl.ds(pl.multiple_of(i * BLK, BLK), BLK)
        new, gqs = [], []
        cos, sin, _ = tables(tab_ref[rows, :])
        for e in range(2):
            s_content, s_pos, s_proj = carry[e]
            g = gq_s[e, rows, :] * (DH**-0.5)
            turned = jnp.concatenate(
                [(g * cos).astype(BF), (g * sin).astype(BF)], 1
            )
            swapped = jnp.concatenate([mat_ref[0, e, DH:, :], mat_ref[0, e, :DH, :]], 0)
            gqp = dot(turned, swapped, 1, 1)
            gqs.append(g + gqp)
            s_content = s_content + jnp.sum(g, axis=0, keepdims=True)
            s_pos = s_pos + jnp.sum(gqp, axis=0, keepdims=True)
            s_proj = s_proj + dot(both_s[e, rows, :], turned, 0, 0)
            new.append((s_content, s_pos, s_proj))
        res_s[0, rows, :] = jnp.where(first, gqs[0], pltpu.roll(gqs[1], DH, 1))
        return tuple(new)

    row0 = jnp.zeros((1, 128), F32)
    zero = (row0, row0, jnp.zeros((128, 256), F32))
    sums = lax.fori_loop(0, nb, finish, (zero, zero), unroll=True)
    for e in range(2):
        gsm_ref[0, e, 0:1, :] = sums[e][0]
        gsm_ref[0, e, 1:2, :] = sums[e][1]
        gpp_ref[0, e] = sums[e][2]

    for at in range(width3 // 128):

        @pl.when(p == at)
        def _(at=at):
            for part in range(3):
                off = part * width3 + at * 128
                gqkv_ref[0, :, off : off + 128] = res_s[part].astype(BF)


def attention_specs(L, width):
    pairs = width // 128
    pair = lambda k: pl.BlockSpec((1, L, 128), lambda m, p, *_: (m, 0, k * pairs + p))
    per_m = lambda *s: pl.BlockSpec((1,) + s, lambda m, p, *_: (m,) + (0,) * len(s))
    per_p = lambda *s: pl.BlockSpec((1,) + s, lambda m, p, *_: (p,) + (0,) * len(s))
    whole = lambda *s: pl.BlockSpec(s, lambda m, p, *_: (0,) * len(s))
    return pairs, pair, per_m, per_p, whole


def attention_forward(qkv, lohi, segr, tab, bias, mat, vb):
    M, L, w3 = qkv.shape
    width = w3 // 3
    nb = L // BLK
    pairs, pair, per_m, per_p, whole = attention_specs(L, width)
    return pl.pallas_call(
        fwd_kernel,
        out_shape=(
            jax.ShapeDtypeStruct((M, L, width), BF),
            jax.ShapeDtypeStruct((M, L, width), BF),
            jax.ShapeDtypeStruct((M, pairs, 2, L // 128, 1, 128), F32),
        ),
        grid_spec=pltpu.PrefetchScalarGridSpec(
            num_scalar_prefetch=1,
            grid=(M, pairs),
            in_specs=[
                pair(0), pair(1), pair(2), per_m(L // 128, 1, 128), whole(L, 128), per_p(2, 128),
                per_p(2, 128, 256), per_p(1, 128),
            ],
            out_specs=[
                pair(0), pair(0),
                pl.BlockSpec((1, 1, 2, L // 128, 1, 128), lambda m, p, *_: (m, p, 0, 0, 0, 0)),
            ],
            scratch_shapes=[
                pltpu.VMEM((2, L, 128), BF),
                pltpu.VMEM((2, L, 128), BF),
                pltpu.VMEM((L, 128), F32),
            ],
        ),
        compiler_params=pltpu.CompilerParams(
            dimension_semantics=("arbitrary", "arbitrary"), vmem_limit_bytes=32 << 20
        ),
        name="attend",
    )(lohi, qkv, qkv, qkv, segr, tab, bias, mat, vb)


def attention_backward(m, into, qkv, g, o, lse, lohi, segr, tab, bias, mat):
    M, L, w3 = qkv.shape
    more = [] if into is None else [into]
    width = w3 // 3
    pairs = width // 128
    pair = lambda k: pl.BlockSpec((1, L, 128), lambda p, *_: (m, 0, k * pairs + p))
    per_m = lambda *s: pl.BlockSpec((1,) + s, lambda p, *_: (m,) + (0,) * len(s))
    per_p = lambda *s: pl.BlockSpec((1,) + s, lambda p, *_: (p,) + (0,) * len(s))
    whole = lambda *s: pl.BlockSpec(s, lambda p, *_: (0,) * len(s))
    return pl.pallas_call(
        functools.partial(bwd_kernel, m),
        out_shape=(
            jax.ShapeDtypeStruct((M, L, w3), BF),
            jax.ShapeDtypeStruct((pairs, 2, 8, 128), F32),
            jax.ShapeDtypeStruct((pairs, 2, 128, 256), F32),
        ),
        grid_spec=pltpu.PrefetchScalarGridSpec(
            num_scalar_prefetch=1,
            grid=(pairs,),
            in_specs=[
                pair(0), pair(1), pair(2), pair(0), pair(0),
                pl.BlockSpec((1, 1, 2, L // 128, 1, 128), lambda p, *_: (m, p, 0, 0, 0, 0)),
                per_m(L // 128, 1, 128),
                whole(L, 128), per_p(2, 128), per_p(2, 128, 256),
            ] + [pl.BlockSpec(memory_space=pl.ANY) for _ in more],
            out_specs=[per_m(L, w3), per_p(2, 8, 128), per_p(2, 128, 256)],
            scratch_shapes=[
                pltpu.VMEM((2, L, 128), BF),
                pltpu.VMEM((2, L, 128), BF),
                pltpu.VMEM((2, L, 128), BF),
                pltpu.VMEM((L, 128), F32),
                pltpu.VMEM((2, L // 128, 1, 128), F32),
                pltpu.VMEM((2, L, 128), F32),
                pltpu.VMEM((3, L, 128), F32),
            ],
        ),
        compiler_params=pltpu.CompilerParams(
            dimension_semantics=("arbitrary",), vmem_limit_bytes=32 << 20
        ),
        input_output_aliases={11: 0} if more else {},
        name="attend_back",
    )(lohi, qkv, qkv, qkv, g, o, lse, segr, tab, bias, mat, *more)


UB = 512


def ff_forward_kernel(
    hid_ref, hid2_ref, wi_ref, wo_ref, ib_ref, act_ref, dg_ref, own_ref, send_ref, acc
):
    u = pl.program_id(0)
    n2 = 2 * hid_ref.shape[0]
    RB = n2 // 2
    for r in range(n2 // RB):
        rows = slice(r * RB, (r + 1) * RB)
        v = dot((hid_ref if r == 0 else hid2_ref)[...], wi_ref[...]) + ib_ref[...]
        c = math.sqrt(2.0 / math.pi)
        v2 = v * v
        t = jnp.tanh(c * v * (1.0 + 0.044715 * v2))
        h = 0.5 * (1.0 + t)
        act = (v * h).astype(BF)
        dg = h + (0.5 * c) * v * (1.0 - t * t) * (1.0 + (3 * 0.044715) * v2)
        act_ref[rows, :] = act
        dg_ref[rows, :] = dg.astype(BF)
        new = dot(act, wo_ref[...])

        @pl.when(u == 0)
        def _(rows=rows, new=new):
            acc[rows, :] = new

        @pl.when(u > 0)
        def _(rows=rows, new=new):
            acc[rows, :] = acc[rows, :] + new

    @pl.when(u == pl.num_programs(0) - 1)
    def _():
        own_ref[...] = acc[: n2 // 2, :]
        send_ref[...] = acc[n2 // 2 :, :].astype(BF)


def ff_backward_kernel(
    go_ref, hid_ref, hid2_ref, wi_ref, wo_ref, dg_ref, ga_ref, gb_ref, gib_ref, own_ref,
    send_ref, acc, hid_t, gi_s,
):
    u = pl.program_id(0)
    n2 = go_ref.shape[0]
    RB = n2 // 2

    @pl.when(u == 0)
    def _():
        hid_t[:, : n2 // 2] = hid_ref[...].T
        hid_t[:, n2 // 2 :] = hid2_ref[...].T

    total = jnp.zeros((1, UB), F32)
    for r in range(n2 // RB):
        rows = slice(r * RB, (r + 1) * RB)
        gi = (dot(go_ref[rows, :], wo_ref[...], 1, 1) * dg_ref[rows, :].astype(F32)).astype(BF)
        gi_s[rows, :] = gi
        total = total + jnp.sum(gi.astype(F32), axis=0, keepdims=True)
        new = dot(gi, wi_ref[...], 1, 1)

        @pl.when(u == 0)
        def _(rows=rows, new=new):
            acc[rows, :] = new

        @pl.when(u > 0)
        def _(rows=rows, new=new):
            acc[rows, :] = acc[rows, :] + new

    gib_ref[...] = total
    g = dot(hid_t[...], gi_s[...]).astype(BF)

    @pl.when(u < pl.num_programs(0) // 2)
    def _():
        ga_ref[...] = g

    @pl.when(u >= pl.num_programs(0) // 2)
    def _():
        gb_ref[...] = g

    @pl.when(u == pl.num_programs(0) - 1)
    def _():
        own_ref[...] = acc[: n2 // 2, :]
        send_ref[...] = acc[n2 // 2 :, :].astype(BF)


def ff_specs(n2, d, fh):
    nq = fh // 2 // UB
    fixed = lambda *shape: pl.BlockSpec(shape, lambda u: (0,) * len(shape))
    units = lambda rows: pl.BlockSpec((rows, UB), lambda u: (0, u))
    outer = pl.BlockSpec((UB, d), lambda u: (lax.rem(u, nq), fh // d + u // nq))
    return fixed, units, outer


def ff_forward(hid, hid2, big, ib, fh):
    n2, d = 2 * hid.shape[0], hid.shape[1]
    fixed, units, outer = ff_specs(n2, d, fh)
    return pl.pallas_call(
        ff_forward_kernel,
        out_shape=(
            jax.ShapeDtypeStruct((n2, fh), BF),
            jax.ShapeDtypeStruct((n2, fh), BF),
            jax.ShapeDtypeStruct((n2 // 2, d), F32),
            jax.ShapeDtypeStruct((n2 // 2, d), BF),
        ),
        grid=(fh // UB,),
        in_specs=[fixed(n2 // 2, d), fixed(n2 // 2, d), units(d), outer, units(1)],
        out_specs=[units(n2), units(n2), fixed(n2 // 2, d), fixed(n2 // 2, d)],
        scratch_shapes=[pltpu.VMEM((n2, d), F32)],
        compiler_params=pltpu.CompilerParams(
            dimension_semantics=("arbitrary",), vmem_limit_bytes=56 << 20
        ),
        name="feed",
    )(hid, hid2, big, big, ib)


def ff_backward(go, hid, hid2, big, dg, fh):
    n2, d = go.shape
    fixed, units, outer = ff_specs(n2, d, fh)
    nq = fh // 2 // UB
    return pl.pallas_call(
        ff_backward_kernel,
        out_shape=(
            jax.ShapeDtypeStruct((d, fh // 2), BF),
            jax.ShapeDtypeStruct((d, fh // 2), BF),
            jax.ShapeDtypeStruct((1, fh), F32),
            jax.ShapeDtypeStruct((n2 // 2, d), F32),
            jax.ShapeDtypeStruct((n2 // 2, d), BF),
        ),
        grid=(fh // UB,),
        in_specs=[
            fixed(n2, d), fixed(n2 // 2, d), fixed(n2 // 2, d), units(d), outer, units(n2),
        ],
        out_specs=[
            pl.BlockSpec((d, UB), lambda u: (0, jnp.minimum(u, nq - 1))),
            pl.BlockSpec((d, UB), lambda u: (0, jnp.maximum(u - nq, 0))),
            units(1), fixed(n2 // 2, d), fixed(n2 // 2, d),
        ],
        scratch_shapes=[
            pltpu.VMEM((n2, d), F32),
            pltpu.VMEM((d, n2), BF),
            pltpu.VMEM((n2, UB), BF),
        ],
        compiler_params=pltpu.CompilerParams(
            dimension_semantics=("arbitrary",), vmem_limit_bytes=44 << 20
        ),
        name="feed_back",
    )(go, hid, hid2, big, big, dg)


def per_device(
    tokens, segment_ids, cotangent, query_proj, key_proj, value_proj, out_proj, value_bias,
    content_bias, position_bias, position_proj, out_bias, attn_gain, attn_shift, inner_proj,
    inner_bias, outer_proj, outer_bias, final_gain, final_shift,
):
    M, _, T, D = tokens.shape
    n_dz, n_dx, n_yy, n_core = (lax.axis_size(a) for a in ALL)
    S = n_yy * n_core
    chips = n_dz * n_dx * n_yy
    devices = chips * n_core
    L = T * S
    R = query_proj.shape[0]
    U = outer_proj.shape[0]
    FF = U * devices
    hl = H // S
    width = hl * DH
    pairs = width // 128
    half = DH // 2
    N = M * T
    core = lax.axis_index("core")
    seq = lax.axis_index("yy") * n_core + core
    x_bit = [("dx", 1)]
    yy_bits = [("yy", b) for b in bits_of("yy")]
    two = lambda bits: (2,) * len(bits)

    x = tokens[:, 0]
    x_other = swap(x, "yy", yy_bits[0][1])
    docs = lax.all_gather(segment_ids[:, 0], SEQ, axis=1, tiled=True)
    gate = [x_other]
    by_seq = jnp.stack([query_proj, key_proj, value_proj], 0).reshape(3, R, S, width)
    w3 = 3 * width
    by_seq = by_seq.transpose(2, 1, 0, 3).reshape(S, R, w3)
    mixed = lax.all_to_all(by_seq, SEQ, split_axis=0, concat_axis=0, tiled=True)
    mixed = gather_bits(mixed, "dz", 0, gate)
    w_qkv = gather_bits(mixed, "dx", 1).reshape(D, w3)

    row = lambda v: jnp.pad(v, (0, 128 - v.size))
    vectors = [
        content_bias, position_bias, value_bias, out_bias, attn_gain, attn_shift, outer_bias,
        final_gain, final_shift, inner_bias,
    ]
    n_vec = len(vectors)
    packed = jnp.concatenate([jnp.stack([row(v) for v in vectors]), position_proj.reshape(-1, 128)])
    n_pack = packed.shape[0]
    for axis in reversed(ALL):
        packed = gather_bits(packed, axis)
    packed = packed.reshape(devices, n_pack, 128)
    heads = lambda v: lax.dynamic_slice_in_dim(v.reshape(S, -1), seq, 1, 0)
    full = [packed[:, k, :R] for k in range(n_vec - 1)]
    full_content, full_posbias, full_vbias = full[:3]
    full_posproj = packed[:, n_vec:].reshape(devices, -1)
    vec = lambda v: v.reshape(1, -1).astype(F32)
    full_obias, full_again, full_ashift, full_fbias, full_fgain, full_fshift = map(vec, full[3:9])
    ib = packed[:, n_vec - 1, :U].reshape(chips, n_core, 2, U // 2)
    ib = lax.dynamic_index_in_dim(ib, core, 1, False)
    full_ibias = ib.transpose(1, 0, 2).reshape(1, -1).astype(F32)

    x_all = x
    for k, (axis, bit) in enumerate(yy_bits):
        x_all = double(x_all, axis, bit, 1 + k, x_other if k == 0 else None)
    x_all = x_all.reshape(M, n_yy, T, D)
    x_all = double(x_all, "core", 1, 2).reshape(M * L, D)

    FH, DC = FF // n_core, D // n_core
    inner_cols = inner_proj.reshape(R, chips, n_core, 2, U // 2).transpose(2, 0, 3, 1, 4)
    out_cols = out_proj.reshape(R, n_core, DC).transpose(1, 0, 2)
    cols = jnp.concatenate([inner_cols.reshape(n_core, R, FH), out_cols], 2)
    cols = lax.all_to_all(cols, "core", split_axis=0, concat_axis=0, tiled=True)
    cols = cols.reshape(n_core * R, FH + DC)
    big = [cols[:, :FH], outer_proj[: U // 2], outer_proj[U // 2 :], cols[:, FH:]]
    big = after(jnp.concatenate(big, 1), gate[1], docs)
    big = lax.all_gather(big, CHIP, axis=0, tiled=True)
    w_out_half = big[:, FH + 2 * D :]
    w_out_other = swap(w_out_half, "core", 1)
    by_core = lambda mine, other: jnp.where(
        core == 0, jnp.concatenate([mine, other], 1), jnp.concatenate([other, mine], 1)
    )

    nb = L // BLK
    ends = docs.reshape(M, nb, BLK)
    lo = jnp.sum(docs[:, None, :] < ends[:, :, :1], -1) // 128
    count = (jnp.sum(docs[:, None, :] <= ends[:, :, -1:], -1) - lo * 128 + BLK - 1) // BLK
    lo = jnp.minimum(lo, (L - count * BLK) // 128)
    lohi = jnp.stack([lo, count], -1).reshape(-1).astype(jnp.int32)
    segr = docs.reshape(M, L // 128, 1, 128).astype(F32)
    cos_t, sin_t = rotations(L, half)
    tab = jnp.concatenate([sin_t, sin_t, cos_t, cos_t], 1)
    bias = jnp.stack(
        [heads(full_content).reshape(hl, DH), heads(full_posbias).reshape(hl, DH)], 1
    )
    bias = bias.reshape(pairs, 2, 2 * DH).astype(F32)
    pp = heads(full_posproj).reshape(hl, DH, DH)
    pc, ps = pp[..., :half], pp[..., half:]
    z64 = jnp.zeros((hl, DH, DH), BF)
    mat = jnp.concatenate([z64, pc, -ps, z64, ps, pc], 2)
    mat = jnp.concatenate([jnp.zeros_like(mat), mat], 1).reshape(pairs, 2, 128, 256)
    vb = heads(full_vbias).reshape(pairs, 1, 128).astype(F32)

    qkv = dot(x_all, w_qkv).astype(BF).reshape(M, L, w3)
    ctx, o, lse = attention_forward(qkv, lohi, segr, tab, bias, mat, vb)
    ctx_tok = lax.all_to_all(
        ctx.reshape(M, S, T, width), SEQ, split_axis=1, concat_axis=1, tiled=True
    )
    ctx_tok = ctx_tok.transpose(0, 2, 1, 3).reshape(N, H * DH)
    x_float = x.reshape(N, D).astype(F32)
    attn = by_core(dot(ctx_tok, w_out_half), dot(ctx_tok, w_out_other)) + full_obias
    hidden, first_back = jax.vjp(
        lambda a, g, b: layer_norm(a, g, b), x_float + attn, full_again, full_ashift
    )
    hid = hidden.astype(BF)
    hid2 = swap(hid, "core", 1)
    active, dgelu, part, part_send = ff_forward(hid, hid2, big, full_ibias, FH)
    outer = part + swap(part_send, "core", 1).astype(F32) + full_fbias
    result, second_back = jax.vjp(
        lambda a, g, b: layer_norm(a, g, b), hidden + outer, full_fgain, full_fshift
    )
    output = result.astype(BF).reshape(M, 1, T, D)

    g_hidden, g_fgain, g_fshift = second_back(cotangent[:, 0].reshape(N, D).astype(F32))
    go = g_hidden.astype(BF)
    w_out = by_core(w_out_half, w_out_other)
    go_pair = jnp.concatenate([go, after(swap(go, "core", 1), w_out)], 0)
    FQ = FH // 2
    z_dims = [("dz", b) for b in bits_of("dz")]
    z_bits = z_dims[::-1]
    chip_bits = z_dims + x_bit + yy_bits
    rows = two(chip_bits) + (n_core * R,)
    g_outer_w = [dot(active[:, k * FQ : (k + 1) * FQ], go_pair, 0, 0).astype(BF) for k in range(2)]
    outer_y, outer_x = [Chain([g.reshape(rows + (D,))], chip_bits) for g in g_outer_w]
    outer_y.run(yy_bits[:1])
    outer_x.run(x_bit)
    *g_inner_w, g_ib, g_part, g_send = ff_backward(
        after(go_pair, outer_y.sends[0], outer_x.sends[0]), hid, hid2, big, dgelu, FH
    )
    g_send = meet(g_send, outer_y, outer_x)
    inner_y, inner_x = [
        Chain([g.reshape(rows + (FQ,))], chip_bits) for g in g_inner_w
    ]
    inner_x.run(x_bit)
    inner_y.run(yy_bits[:1])
    g_send = after(g_send, inner_x.sends[0], inner_y.sends[0])
    g_hidden = g_hidden + g_part + swap(g_send, "core", 1).astype(F32)
    g_sum, g_again, g_ashift = first_back(g_hidden)
    ga = g_sum.astype(BF)
    gc = jnp.stack(
        [dot(ga, w_out[k * width : (k + 1) * width], 1, 1).astype(BF) for k in range(S)]
    )
    g_heads = lax.all_to_all(gc, SEQ, split_axis=0, concat_axis=0, tiled=True)
    g_heads = g_heads.reshape(S, M, T, width).transpose(1, 0, 2, 3).reshape(M, L, width)

    ga_cols = after(ga, gc)
    cols = lambda k: lax.dynamic_slice_in_dim(ga_cols, k * DC, DC, 1)
    theirs = swap(dot(ctx_tok, cols(1 - core), 0, 0).astype(BF), "core", 1)
    g_out_half = (dot(ctx_tok, cols(core), 0, 0) + theirs.astype(F32)).astype(BF)
    out_y = Chain([g_out_half.reshape(rows + (DC,))], chip_bits)
    outer_y.terms, outer_x.terms, _ = lax.optimization_barrier((outer_y.terms, outer_x.terms, gc))
    outer_y.run(yy_bits[1:] + x_bit)
    outer_x.run(yy_bits)
    g_heads = meet(after(g_heads, outer_y.sends[-1], outer_x.sends[1]), inner_x, inner_y)
    inner_y.run(yy_bits[1:] + x_bit)
    inner_x.run(yy_bits)
    g_heads = after(g_heads, inner_y.sends[-1], inner_x.sends[1])
    out_y.run(yy_bits)

    gqkv, small = None, []
    for m in range(M):
        gqkv, sm, pp_m = attention_backward(
            m, gqkv, qkv, g_heads, o, lse, lohi, segr, tab, bias, mat
        )
        small.append((sm, pp_m))
        if m == 0:
            gqkv, g_heads = lax.optimization_barrier((gqkv, g_heads))
            g_heads = meet(g_heads, outer_y, outer_x, inner_y, inner_x)
            ff = [outer_y, outer_x, inner_y, inner_x]
            g_heads = after(g_heads, *run_together(ff, z_bits[:1]))
    gqkv = meet(gqkv, out_y, *ff).reshape(M * L, w3)
    gqkv = after(gqkv, *run_together(ff, z_bits[1:]))

    g_qkv_w = dot(x_all, gqkv, 0, 0).astype(BF).reshape(two(z_dims + x_bit) + (S * R, w3))
    mixed = Chain([g_qkv_w], z_dims + x_bit)
    mixed.run(x_bit)
    out_y.run(x_bit)
    dx = after(gqkv, mixed.sends[0], out_y.sends[-1])
    dx = dot(dx, w_qkv, 1, 1).astype(BF).reshape((M,) + two(yy_bits) + (2, T, D))
    dx = jnp.moveaxis(dx, 0, len(yy_bits) + 1)
    dx = Chain([dx], yy_bits + [("core", 1)]).run([("core", 1)] + yy_bits)
    colsums = (gc, ga, go, g_again, g_ashift, g_fgain, g_fshift, g_ib)
    (small, colsums, _) = meet((small, colsums, dx.sends[-1]), mixed, out_y, *ff)
    mixed.run(z_bits)
    out_y.terms = after(out_y.terms, mixed.sends[-1])
    out_y.run(z_bits)
    gc, ga, go, g_again, g_ashift, g_fgain, g_fshift, g_ib = colsums
    gsm, gpp = sum(k[0] for k in small), sum(k[1] for k in small)
    g_mixed = meet(mixed.result().astype(BF), dx)
    g_rows = lax.all_to_all(
        g_mixed.reshape(S, R, 3, width), SEQ, split_axis=0, concat_axis=0, tiled=True
    )
    g_rows = g_rows.astype(F32).transpose(2, 1, 0, 3).reshape(3, R, D)
    input_grad = (g_sum.reshape(M, T, D) + dx.result()).reshape(M, 1, T, D)

    colsum = lambda v: jnp.sum(v.astype(F32), axis=0).reshape(-1)
    gsm = gsm[:, :, :2, :DH].reshape(hl, 2, DH).transpose(1, 0, 2).reshape(2, 1, width)
    here = (jnp.arange(S) == seq).reshape(1, S, 1)
    g_heads_sm = jnp.where(here, gsm, 0.0).reshape(2, D)
    g_rest = [jnp.sum(gc.astype(F32), 1).reshape(-1), colsum(ga)] + [v.reshape(-1) for v in (g_again, g_ashift)]
    g_rest += [colsum(go), g_fgain.reshape(-1), g_fshift.reshape(-1)]
    g_vectors = jnp.concatenate([g_heads_sm, jnp.stack(g_rest)]).astype(BF)
    g_vectors = g_vectors.reshape(n_vec - 1, devices, R).transpose(1, 0, 2)
    g_vectors = jnp.pad(g_vectors, ((0, 0), (0, 0), (0, 128 - R)))
    g_ibias = g_ib.reshape(2, chips, 1, U // 2).transpose(1, 2, 0, 3).reshape(chips, 1, U)
    on_core = (jnp.arange(n_core) == core).reshape(1, n_core, 1)
    g_ibias = jnp.where(on_core, g_ibias, 0.0).reshape(devices, 1, U).astype(BF)
    g_ibias = jnp.pad(g_ibias, ((0, 0), (0, 0), (0, 128 - U)))
    gpp = gpp.reshape(hl, 128, 256)[:, DH:]
    e1, e2 = gpp[:, :, DH : 2 * DH], gpp[:, :, 3 * DH :]
    g_posproj = jnp.concatenate(
        [e1[..., :half] + e2[..., half:], e2[..., :half] - e1[..., half:]], -1
    ).astype(BF)
    g_posproj = jnp.where(here, g_posproj.reshape(1, 1, -1), jnp.zeros((), BF))
    g_posproj = g_posproj.reshape(devices, -1, 128)
    g_packed = jnp.concatenate([g_vectors, g_ibias, g_posproj], 1)
    g_packed = lax.all_to_all(g_packed, ALL, split_axis=0, concat_axis=0, tiled=True)
    g_packed = jnp.sum(g_packed.astype(F32), 0)
    s = [g_packed[k, : v.size] for k, v in enumerate(vectors)]
    g_pp = g_packed[n_vec:].reshape(R, DH)

    outer_grad = jnp.concatenate([outer_y.result(), outer_x.result()], 0)

    def by_rows(v):
        v = v.astype(BF).reshape(n_core, R, -1)
        mine = lax.dynamic_index_in_dim(v, core, 0, False)
        other = swap(lax.dynamic_index_in_dim(v, 1 - core, 0, False), "core", 1)
        return jnp.where(core == 0, mine, other), jnp.where(core == 0, other, mine)

    inner_grad = jnp.stack(by_rows(jnp.concatenate([inner_y.result(), inner_x.result()], 1)), 1)
    inner_grad = inner_grad.reshape(R, n_core, 2, chips, U // 2).transpose(0, 3, 1, 2, 4)
    inner_grad = inner_grad.astype(F32).reshape(R, FF)
    out_grad = jnp.concatenate(by_rows(out_y.result()), 1).astype(F32)

    return (
        output, input_grad, g_rows[0], g_rows[1], g_rows[2], out_grad, s[2], s[0], s[1], g_pp,
        s[3], s[4], s[5], inner_grad, s[9], outer_grad, s[6], s[7], s[8],
    )


def solution(mesh):
    n_dp, n_seq = mesh.devices.shape
    mesh = Mesh(mesh.devices.reshape(n_dp // 2, 2, n_seq // 2, 2), ALL)
    tok, ids = P(None, DP, SEQ, None), P(None, DP, SEQ)
    mat, vec = P(ALL, None), P(ALL)
    in_specs = (
        tok, ids, tok, mat, mat, mat, mat, vec, vec, vec, mat, vec, vec, vec, mat, vec, mat, vec,
        vec, vec,
    )
    out_specs = (
        tok, tok, mat, mat, mat, mat, vec, vec, vec, mat, vec, vec, vec, mat, vec, mat, vec, vec,
        vec,
    )
    return jax.shard_map(
        per_device, mesh=mesh, in_specs=in_specs, out_specs=out_specs, check_vma=False
    )
```

```python
import functools
import math

import jax
import jax.numpy as jnp
from jax import lax
from jax.experimental import pallas as pl
from jax.experimental.pallas import tpu as pltpu
from jax.sharding import Mesh, PartitionSpec as P

H = 16
DH = 64
BLK = 256
GRP = 2
NEG = -1e30
BF = jnp.bfloat16
F32 = jnp.float32
DP = ("dz", "dx")
SEQ = ("yy", "core")
CHIP = DP + ("yy",)
ALL = DP + SEQ


def dot(a, b, ca=1, cb=0):
    return lax.dot_general(a, b, (((ca,), (cb,)), ((), ())), preferred_element_type=F32)


def rotations(length, half_size):
    position = jnp.arange(length, dtype=jnp.int32).astype(F32)
    steps = jnp.arange(half_size, dtype=jnp.int32).astype(F32)
    frequency = jnp.exp(steps * (-math.log(10000.0) / half_size))
    angle = position[:, None] * frequency[None, :]
    return (jnp.cos(angle), jnp.sin(angle))


def layer_norm(values, gain, shift):
    average = jnp.mean(values, axis=-1, keepdims=True)
    centred = values - average
    variance = jnp.mean(centred * centred, axis=-1, keepdims=True)
    return centred * lax.rsqrt(variance + 1e-06) * gain + shift


def gelu_tanh(values):
    return jax.nn.gelu(values, approximate=True)


def swap(x, axis, bit):
    n = lax.axis_size(axis)
    return lax.ppermute(x, axis, [(i, i ^ bit) for i in range(n)])


def side(axis, bit):
    return jnp.where((lax.axis_index(axis) & bit) != 0, 1, 0)


def double(x, axis, bit, dim, other=None):
    other = swap(x, axis, bit) if other is None else other
    mine = side(axis, bit) == 0
    return jnp.stack([jnp.where(mine, x, other), jnp.where(mine, other, x)], dim)


def bits_of(axis):
    n = lax.axis_size(axis)
    return [1 << k for k in reversed(range(n.bit_length() - 1))]


def gather_bits(x, axis, dim=0, wait=None):
    bits = bits_of(axis)
    for k, bit in enumerate(bits):
        x = double(x, axis, bit, dim + k)
        if wait is not None and k == 0:
            behind = tuple(wait)
            wait.append(x)
            x = after(x, *behind)
    return x.reshape(x.shape[:dim] + (lax.axis_size(axis),) + x.shape[dim + len(bits) :])


def total(terms):
    return sum(t.astype(F32) for t in terms)


class Chain:
    def __init__(self, terms, left):
        self.terms, self.left, self.sends = terms, list(left), []

    def send(self, step):
        axis, bit = step
        dim = self.left.index(step)
        self.left.pop(dim)
        mine = side(axis, bit)
        take = lambda t, k: lax.dynamic_index_in_dim(t, k, dim, keepdims=False)
        out = total([take(t, 1 - mine) for t in self.terms]).astype(BF)
        self.terms = [take(t, mine) for t in self.terms]
        self.sends.append(out)
        return out

    def run(self, steps):
        for step in steps:
            got = swap(self.send(step), *step)
            self.terms.append(got)
        return self

    def result(self):
        return total(self.terms)


def send_together(chains, step):
    return jnp.concatenate([c.send(step) for c in chains], -1)


def take_together(chains, got):
    at = 0
    for c in chains:
        width = c.terms[0].shape[-1]
        c.terms.append(got[..., at : at + width])
        at += width


def run_together(chains, steps):
    sends = []
    for step in steps:
        sends.append(send_together(chains, step))
        take_together(chains, swap(sends[-1], *step))
    return sends


def after(x, *others):
    return lax.optimization_barrier((x,) + others)[0]


def meet(x, *chains):
    x, last = lax.optimization_barrier((x, [c.terms[-1] for c in chains]))
    for c, t in zip(chains, last):
        c.terms[-1] = t
    return x


def tables(tab):
    lane = lax.broadcasted_iota(jnp.int32, tab.shape, 1)
    turned = pltpu.roll(tab, DH, 1)
    cos = jnp.where(lane < DH, 0.0, tab)
    sin = jnp.where(lane < DH, 0.0, turned)
    return cos, sin, jnp.where(lane < DH + DH // 2, tab, turned)


def prep_head(e, q, qr, k, kr, first, bias, mat, cos, sin, pk):
    base = jnp.where(first, q, qr) if e == 0 else jnp.where(first, qr, q)
    both = (base + bias).astype(BF)
    turned = dot(both, mat)
    rel = turned[:, :128] * cos + turned[:, 128:] * sin
    qf = (jnp.where(first, both.astype(F32), rel) * (DH**-0.5)).astype(BF)
    kf = jnp.where(first, k if e == 0 else kr, pk).astype(BF)
    return both, qf, kf


def row_of(ref, start, width):
    return jnp.concatenate([ref[0, start + t] for t in range(width // 128)], 1)


def seg_columns(segr_ref, seg_s, i):
    for t in range(i * (BLK // 128), (i + 1) * (BLK // 128)):
        tile = jnp.broadcast_to(segr_ref[0, t], (128, 128)).T
        seg_s[t * 128 : (t + 1) * 128, :] = tile


def by_width(n, most, body):
    for k in range(1, most + 1):

        @pl.when(n == k)
        def _(k=k):
            body(k * BLK)


def fwd_kernel(
    lohi, q_ref, k_ref, v_ref, segr_ref, tab_ref, bias_ref, mat_ref, vb_ref,
    ctx_ref, o_ref, lse_ref, qf_s, kf_s, seg_s,
):
    m = pl.program_id(0)
    nb = q_ref.shape[1] // BLK
    first = lax.broadcasted_iota(jnp.int32, (BLK, 128), 1) < DH

    def prep(i):
        rows = slice(i * BLK, (i + 1) * BLK)
        seg_columns(segr_ref, seg_s, i)
        q = q_ref[0, rows, :].astype(F32)
        k = k_ref[0, rows, :].astype(F32)
        qr, kr = pltpu.roll(q, DH, 1), pltpu.roll(k, DH, 1)
        cos, sin, pk = tables(tab_ref[rows, :])
        for e in range(2):
            _, qf, kf = prep_head(
                e, q, qr, k, kr, first, bias_ref[0, e : e + 1, :], mat_ref[0, e],
                cos, sin, pk,
            )
            qf_s[e, rows, :] = qf
            kf_s[e, rows, :] = kf

    for i in range(nb):
        prep(i)

    def q_group(i, c):
        at = (m * nb + i * GRP) * 2
        starts = [lohi[at + 2 * u] for u in range(GRP)]
        n = lohi[at + 1]
        for u in range(1, GRP):
            n = jnp.maximum(n, lohi[at + 2 * u + 1])

        def body(width):
            for u in range(GRP):
                rows = pl.ds(pl.multiple_of((i * GRP + u) * BLK, BLK), BLK)
                start = jnp.minimum(starts[u], (nb * BLK - width) // 128)
                cols = pl.ds(pl.multiple_of(start * 128, 128), width)
                segq = jnp.concatenate([seg_s[rows, :]] * (width // 128), 1)
                same = segq == row_of(segr_ref, start, width)
                outs = []
                for e in range(2):
                    s = dot(qf_s[e, rows, :], kf_s[e, cols, :], 1, 1)
                    s = jnp.where(same, s, NEG)
                    top = jnp.max(s, axis=1, keepdims=True)
                    p = jnp.exp(s - top)
                    total = jnp.sum(p, axis=1, keepdims=True)
                    acc = dot(p.astype(BF), v_ref[0, cols, :])
                    outs.append((acc / total, top + jnp.log(total)))
                o = jnp.where(first, outs[0][0], outs[1][0])
                o_ref[0, rows, :] = o.astype(BF)
                lse_t = jnp.where(first, outs[0][1], outs[1][1]).T
                for e in range(2):
                    for t in range(BLK // 128):
                        lse_ref[0, 0, e, (i * GRP + u) * (BLK // 128) + t] = lse_t[
                            e * DH : e * DH + 1, t * 128 : t * 128 + 128
                        ]
                ctx_ref[0, rows, :] = (o + vb_ref[0]).astype(BF)

        by_width(n, nb, body)
        return c

    lax.fori_loop(0, nb // GRP, q_group, 0)


def bwd_kernel(
    m, lohi, q_ref, k_ref, v_ref, g_ref, o_ref, lse_ref, segr_ref, tab_ref, bias_ref,
    mat_ref, *refs,
):
    gqkv_ref, gsm_ref, gpp_ref, both_s, qf_s, kf_s, seg_s, dl_s, gq_s, res_s = refs[-10:]
    p = pl.program_id(0)
    nb = q_ref.shape[1] // BLK
    width3 = gqkv_ref.shape[2] // 3
    first = lax.broadcasted_iota(jnp.int32, (BLK, 128), 1) < DH

    def prep(i):
        rows = slice(i * BLK, (i + 1) * BLK)
        seg_columns(segr_ref, seg_s, i)
        q = q_ref[0, rows, :].astype(F32)
        k = k_ref[0, rows, :].astype(F32)
        qr, kr = pltpu.roll(q, DH, 1), pltpu.roll(k, DH, 1)
        cos, sin, pk = tables(tab_ref[rows, :])
        dl_t = (g_ref[0, rows, :].astype(F32) * o_ref[0, rows, :].astype(F32)).T
        for e in range(2):
            both, qf, kf = prep_head(
                e, q, qr, k, kr, first, bias_ref[0, e : e + 1, :], mat_ref[0, e],
                cos, sin, pk,
            )
            both_s[e, rows, :] = both
            qf_s[e, rows, :] = qf
            kf_s[e, rows, :] = kf
            gq_s[e, rows, :] = jnp.zeros((BLK, 128), F32)
            dl = jnp.sum(dl_t[e * DH : (e + 1) * DH, :], axis=0, keepdims=True)
            for t in range(BLK // 128):
                dl_s[e, i * (BLK // 128) + t] = dl[:, t * 128 : t * 128 + 128]

    for i in range(nb):
        prep(i)

    def k_group(j, c):
        at = (m * nb + j * GRP) * 2
        starts = [lohi[at + 2 * u] for u in range(GRP)]
        n = lohi[at + 1]
        for u in range(1, GRP):
            n = jnp.maximum(n, lohi[at + 2 * u + 1])

        def body(width):
            for u in range(GRP):
                rows = pl.ds(pl.multiple_of((j * GRP + u) * BLK, BLK), BLK)
                start = jnp.minimum(starts[u], (nb * BLK - width) // 128)
                cols = pl.ds(pl.multiple_of(start * 128, 128), width)
                segk = jnp.concatenate([seg_s[rows, :]] * (width // 128), 1)
                same = segk == row_of(segr_ref, start, width)
                g = g_ref[0, cols, :]
                v = v_ref[0, rows, :].astype(F32)
                outs = []
                for e in range(2):
                    row = lambda ref: jnp.concatenate(
                        [ref[e, start + t] for t in range(width // 128)], 1
                    )
                    mine = first if e == 0 else jnp.logical_not(first)
                    vm = jnp.where(mine, v, 0.0).astype(BF)
                    kf, qf = kf_s[e, rows, :], qf_s[e, cols, :]
                    prob = jnp.where(same, jnp.exp(dot(kf, qf, 1, 1) - row(lse_ref.at[0, 0])), 0.0)
                    ds = (prob * (dot(vm, g, 1, 1) - row(dl_s))).astype(BF)
                    gv = dot(prob.astype(BF), g)
                    gk = dot(ds, qf)
                    gq_s[e, cols, :] = gq_s[e, cols, :] + dot(ds, kf, 0, 0)
                    outs.append((gk, gv))
                res_s[1, rows, :] = jnp.where(first, outs[0][0], pltpu.roll(outs[1][0], DH, 1))
                res_s[2, rows, :] = jnp.where(first, outs[0][1], outs[1][1])

        by_width(n, nb, body)
        return c

    lax.fori_loop(0, nb // GRP, k_group, 0)

    def finish(i, carry):
        rows = pl.ds(pl.multiple_of(i * BLK, BLK), BLK)
        new, gqs = [], []
        cos, sin, _ = tables(tab_ref[rows, :])
        for e in range(2):
            s_content, s_pos, s_proj = carry[e]
            g = gq_s[e, rows, :] * (DH**-0.5)
            turned = jnp.concatenate(
                [(g * cos).astype(BF), (g * sin).astype(BF)], 1
            )
            swapped = jnp.concatenate([mat_ref[0, e, DH:, :], mat_ref[0, e, :DH, :]], 0)
            gqp = dot(turned, swapped, 1, 1)
            gqs.append(g + gqp)
            s_content = s_content + jnp.sum(g, axis=0, keepdims=True)
            s_pos = s_pos + jnp.sum(gqp, axis=0, keepdims=True)
            s_proj = s_proj + dot(both_s[e, rows, :], turned, 0, 0)
            new.append((s_content, s_pos, s_proj))
        res_s[0, rows, :] = jnp.where(first, gqs[0], pltpu.roll(gqs[1], DH, 1))
        return tuple(new)

    row0 = jnp.zeros((1, 128), F32)
    zero = (row0, row0, jnp.zeros((128, 256), F32))
    sums = lax.fori_loop(0, nb, finish, (zero, zero), unroll=True)
    for e in range(2):
        gsm_ref[0, e, 0:1, :] = sums[e][0]
        gsm_ref[0, e, 1:2, :] = sums[e][1]
        gpp_ref[0, e] = sums[e][2]

    for at in range(width3 // 128):

        @pl.when(p == at)
        def _(at=at):
            for part in range(3):
                off = part * width3 + at * 128
                gqkv_ref[0, :, off : off + 128] = res_s[part].astype(BF)


def attention_specs(L, width):
    pairs = width // 128
    pair = lambda k: pl.BlockSpec((1, L, 128), lambda m, p, *_: (m, 0, k * pairs + p))
    per_m = lambda *s: pl.BlockSpec((1,) + s, lambda m, p, *_: (m,) + (0,) * len(s))
    per_p = lambda *s: pl.BlockSpec((1,) + s, lambda m, p, *_: (p,) + (0,) * len(s))
    whole = lambda *s: pl.BlockSpec(s, lambda m, p, *_: (0,) * len(s))
    return pairs, pair, per_m, per_p, whole


def attention_forward(qkv, lohi, segr, tab, bias, mat, vb):
    M, L, w3 = qkv.shape
    width = w3 // 3
    nb = L // BLK
    pairs, pair, per_m, per_p, whole = attention_specs(L, width)
    return pl.pallas_call(
        fwd_kernel,
        out_shape=(
            jax.ShapeDtypeStruct((M, L, width), BF),
            jax.ShapeDtypeStruct((M, L, width), BF),
            jax.ShapeDtypeStruct((M, pairs, 2, L // 128, 1, 128), F32),
        ),
        grid_spec=pltpu.PrefetchScalarGridSpec(
            num_scalar_prefetch=1,
            grid=(M, pairs),
            in_specs=[
                pair(0), pair(1), pair(2), per_m(L // 128, 1, 128), whole(L, 128), per_p(2, 128),
                per_p(2, 128, 256), per_p(1, 128),
            ],
            out_specs=[
                pair(0), pair(0),
                pl.BlockSpec((1, 1, 2, L // 128, 1, 128), lambda m, p, *_: (m, p, 0, 0, 0, 0)),
            ],
            scratch_shapes=[
                pltpu.VMEM((2, L, 128), BF),
                pltpu.VMEM((2, L, 128), BF),
                pltpu.VMEM((L, 128), F32),
            ],
        ),
        compiler_params=pltpu.CompilerParams(
            dimension_semantics=("arbitrary", "arbitrary"), vmem_limit_bytes=32 << 20
        ),
        name="attend",
    )(lohi, qkv, qkv, qkv, segr, tab, bias, mat, vb)


def attention_backward(m, into, qkv, g, o, lse, lohi, segr, tab, bias, mat):
    M, L, w3 = qkv.shape
    more = [] if into is None else [into]
    width = w3 // 3
    pairs = width // 128
    pair = lambda k: pl.BlockSpec((1, L, 128), lambda p, *_: (m, 0, k * pairs + p))
    per_m = lambda *s: pl.BlockSpec((1,) + s, lambda p, *_: (m,) + (0,) * len(s))
    per_p = lambda *s: pl.BlockSpec((1,) + s, lambda p, *_: (p,) + (0,) * len(s))
    whole = lambda *s: pl.BlockSpec(s, lambda p, *_: (0,) * len(s))
    return pl.pallas_call(
        functools.partial(bwd_kernel, m),
        out_shape=(
            jax.ShapeDtypeStruct((M, L, w3), BF),
            jax.ShapeDtypeStruct((pairs, 2, 8, 128), F32),
            jax.ShapeDtypeStruct((pairs, 2, 128, 256), F32),
        ),
        grid_spec=pltpu.PrefetchScalarGridSpec(
            num_scalar_prefetch=1,
            grid=(pairs,),
            in_specs=[
                pair(0), pair(1), pair(2), pair(0), pair(0),
                pl.BlockSpec((1, 1, 2, L // 128, 1, 128), lambda p, *_: (m, p, 0, 0, 0, 0)),
                per_m(L // 128, 1, 128),
                whole(L, 128), per_p(2, 128), per_p(2, 128, 256),
            ] + [pl.BlockSpec(memory_space=pl.ANY) for _ in more],
            out_specs=[per_m(L, w3), per_p(2, 8, 128), per_p(2, 128, 256)],
            scratch_shapes=[
                pltpu.VMEM((2, L, 128), BF),
                pltpu.VMEM((2, L, 128), BF),
                pltpu.VMEM((2, L, 128), BF),
                pltpu.VMEM((L, 128), F32),
                pltpu.VMEM((2, L // 128, 1, 128), F32),
                pltpu.VMEM((2, L, 128), F32),
                pltpu.VMEM((3, L, 128), F32),
            ],
        ),
        compiler_params=pltpu.CompilerParams(
            dimension_semantics=("arbitrary",), vmem_limit_bytes=56 << 20
        ),
        input_output_aliases={11: 0} if more else {},
        name="attend_back",
    )(lohi, qkv, qkv, qkv, g, o, lse, segr, tab, bias, mat, *more)


UB = 512


def ff_forward_kernel(
    hid_ref, hid2_ref, wi_ref, wo_ref, ib_ref, act_ref, dg_ref, own_ref, send_ref, acc
):
    u = pl.program_id(0)
    n2 = 2 * hid_ref.shape[0]
    RB = n2 // 2
    for r in range(n2 // RB):
        rows = slice(r * RB, (r + 1) * RB)
        v = dot((hid_ref if r == 0 else hid2_ref)[...], wi_ref[...]) + ib_ref[...]
        c = math.sqrt(2.0 / math.pi)
        v2 = v * v
        t = jnp.tanh(c * v * (1.0 + 0.044715 * v2))
        h = 0.5 * (1.0 + t)
        act = (v * h).astype(BF)
        dg = h + (0.5 * c) * v * (1.0 - t * t) * (1.0 + (3 * 0.044715) * v2)
        act_ref[rows, :] = act
        dg_ref[rows, :] = dg.astype(BF)
        new = dot(act, wo_ref[...])

        @pl.when(u == 0)
        def _(rows=rows, new=new):
            acc[rows, :] = new

        @pl.when(u > 0)
        def _(rows=rows, new=new):
            acc[rows, :] = acc[rows, :] + new

    @pl.when(u == pl.num_programs(0) - 1)
    def _():
        own_ref[...] = acc[: n2 // 2, :]
        send_ref[...] = acc[n2 // 2 :, :].astype(BF)


def ff_backward_kernel(
    go_ref, hid_ref, hid2_ref, wi_ref, wo_ref, dg_ref, ga_ref, gb_ref, gib_ref, own_ref,
    send_ref, acc, hid_t, gi_s,
):
    u = pl.program_id(0)
    n2 = go_ref.shape[0]
    RB = n2 // 2

    @pl.when(u == 0)
    def _():
        hid_t[:, : n2 // 2] = hid_ref[...].T
        hid_t[:, n2 // 2 :] = hid2_ref[...].T

    total = jnp.zeros((1, UB), F32)
    for r in range(n2 // RB):
        rows = slice(r * RB, (r + 1) * RB)
        gi = (dot(go_ref[rows, :], wo_ref[...], 1, 1) * dg_ref[rows, :].astype(F32)).astype(BF)
        gi_s[rows, :] = gi
        total = total + jnp.sum(gi.astype(F32), axis=0, keepdims=True)
        new = dot(gi, wi_ref[...], 1, 1)

        @pl.when(u == 0)
        def _(rows=rows, new=new):
            acc[rows, :] = new

        @pl.when(u > 0)
        def _(rows=rows, new=new):
            acc[rows, :] = acc[rows, :] + new

    gib_ref[...] = total
    g = dot(hid_t[...], gi_s[...]).astype(BF)

    @pl.when(u < pl.num_programs(0) // 2)
    def _():
        ga_ref[...] = g

    @pl.when(u >= pl.num_programs(0) // 2)
    def _():
        gb_ref[...] = g

    @pl.when(u == pl.num_programs(0) - 1)
    def _():
        own_ref[...] = acc[: n2 // 2, :]
        send_ref[...] = acc[n2 // 2 :, :].astype(BF)


def ff_specs(n2, d, fh):
    nq = fh // 2 // UB
    fixed = lambda *shape: pl.BlockSpec(shape, lambda u: (0,) * len(shape))
    units = lambda rows: pl.BlockSpec((rows, UB), lambda u: (0, u))
    outer = pl.BlockSpec((UB, d), lambda u: (lax.rem(u, nq), fh // d + u // nq))
    return fixed, units, outer


def ff_forward(hid, hid2, big, ib, fh):
    n2, d = 2 * hid.shape[0], hid.shape[1]
    fixed, units, outer = ff_specs(n2, d, fh)
    return pl.pallas_call(
        ff_forward_kernel,
        out_shape=(
            jax.ShapeDtypeStruct((n2, fh), BF),
            jax.ShapeDtypeStruct((n2, fh), BF),
            jax.ShapeDtypeStruct((n2 // 2, d), F32),
            jax.ShapeDtypeStruct((n2 // 2, d), BF),
        ),
        grid=(fh // UB,),
        in_specs=[fixed(n2 // 2, d), fixed(n2 // 2, d), units(d), outer, units(1)],
        out_specs=[units(n2), units(n2), fixed(n2 // 2, d), fixed(n2 // 2, d)],
        scratch_shapes=[pltpu.VMEM((n2, d), F32)],
        compiler_params=pltpu.CompilerParams(
            dimension_semantics=("arbitrary",), vmem_limit_bytes=56 << 20
        ),
        name="feed",
    )(hid, hid2, big, big, ib)


def ff_backward(go, hid, hid2, big, dg, fh):
    n2, d = go.shape
    fixed, units, outer = ff_specs(n2, d, fh)
    nq = fh // 2 // UB
    return pl.pallas_call(
        ff_backward_kernel,
        out_shape=(
            jax.ShapeDtypeStruct((d, fh // 2), BF),
            jax.ShapeDtypeStruct((d, fh // 2), BF),
            jax.ShapeDtypeStruct((1, fh), F32),
            jax.ShapeDtypeStruct((n2 // 2, d), F32),
            jax.ShapeDtypeStruct((n2 // 2, d), BF),
        ),
        grid=(fh // UB,),
        in_specs=[
            fixed(n2, d), fixed(n2 // 2, d), fixed(n2 // 2, d), units(d), outer, units(n2),
        ],
        out_specs=[
            pl.BlockSpec((d, UB), lambda u: (0, jnp.minimum(u, nq - 1))),
            pl.BlockSpec((d, UB), lambda u: (0, jnp.maximum(u - nq, 0))),
            units(1), fixed(n2 // 2, d), fixed(n2 // 2, d),
        ],
        scratch_shapes=[
            pltpu.VMEM((n2, d), F32),
            pltpu.VMEM((d, n2), BF),
            pltpu.VMEM((n2, UB), BF),
        ],
        compiler_params=pltpu.CompilerParams(
            dimension_semantics=("arbitrary",), vmem_limit_bytes=44 << 20
        ),
        name="feed_back",
    )(go, hid, hid2, big, big, dg)


def per_device(
    tokens, segment_ids, cotangent, query_proj, key_proj, value_proj, out_proj, value_bias,
    content_bias, position_bias, position_proj, out_bias, attn_gain, attn_shift, inner_proj,
    inner_bias, outer_proj, outer_bias, final_gain, final_shift,
):
    M, _, T, D = tokens.shape
    n_dz, n_dx, n_yy, n_core = (lax.axis_size(a) for a in ALL)
    S = n_yy * n_core
    chips = n_dz * n_dx * n_yy
    devices = chips * n_core
    L = T * S
    R = query_proj.shape[0]
    U = outer_proj.shape[0]
    FF = U * devices
    hl = H // S
    width = hl * DH
    pairs = width // 128
    half = DH // 2
    N = M * T
    core = lax.axis_index("core")
    seq = lax.axis_index("yy") * n_core + core
    x_bit = [("dx", 1)]
    yy_bits = [("yy", b) for b in bits_of("yy")]
    two = lambda bits: (2,) * len(bits)

    x = tokens[:, 0]
    x_other = swap(x, "yy", yy_bits[0][1])
    docs = lax.all_gather(segment_ids[:, 0], SEQ, axis=1, tiled=True)
    gate = [x_other]
    by_seq = jnp.stack([query_proj, key_proj, value_proj], 0).reshape(3, R, S, width)
    w3 = 3 * width
    by_seq = by_seq.transpose(2, 1, 0, 3).reshape(S, R, w3)
    mixed = lax.all_to_all(by_seq, SEQ, split_axis=0, concat_axis=0, tiled=True)
    z_first = gather_bits(gather_bits(mixed[..., : w3 // 2], "dz", 0, gate), "dx", 1)
    x_first = gather_bits(gather_bits(mixed[..., w3 // 2 :], "dx"), "dz")
    w_qkv = jnp.concatenate([z_first, x_first], -1).reshape(D, w3)

    row = lambda v: jnp.pad(v, (0, 128 - v.size))
    vectors = [
        content_bias, position_bias, value_bias, out_bias, attn_gain, attn_shift, outer_bias,
        final_gain, final_shift, inner_bias,
    ]
    n_vec = len(vectors)
    packed = jnp.concatenate([jnp.stack([row(v) for v in vectors]), position_proj.reshape(-1, 128)])
    n_pack = packed.shape[0]
    packed = jnp.broadcast_to(after(packed, gate[1])[None], (devices, n_pack, 128))
    packed = lax.all_to_all(packed, ALL, split_axis=0, concat_axis=0, tiled=True)
    heads = lambda v: lax.dynamic_slice_in_dim(v.reshape(S, -1), seq, 1, 0)
    full = [packed[:, k, :R] for k in range(n_vec - 1)]
    full_content, full_posbias, full_vbias = full[:3]
    full_posproj = packed[:, n_vec:].reshape(devices, -1)
    vec = lambda v: v.reshape(1, -1).astype(F32)
    full_obias, full_again, full_ashift, full_fbias, full_fgain, full_fshift = map(vec, full[3:9])
    ib = packed[:, n_vec - 1, :U].reshape(chips, n_core, 2, U // 2)
    ib = lax.dynamic_index_in_dim(ib, core, 1, False)
    full_ibias = ib.transpose(1, 0, 2).reshape(1, -1).astype(F32)

    x_all = x
    for k, (axis, bit) in enumerate(yy_bits):
        x_all = double(x_all, axis, bit, 1 + k, x_other if k == 0 else None)
    x_all = x_all.reshape(M, n_yy, T, D)
    x_all = double(x_all, "core", 1, 2).reshape(M * L, D)

    FH, DC = FF // n_core, D // n_core
    inner_cols = inner_proj.reshape(R, chips, n_core, 2, U // 2).transpose(2, 0, 3, 1, 4)
    out_cols = out_proj.reshape(R, n_core, DC).transpose(1, 0, 2)
    cols = jnp.concatenate([inner_cols.reshape(n_core, R, FH), out_cols], 2)
    cols = lax.all_to_all(cols, "core", split_axis=0, concat_axis=0, tiled=True)
    cols = cols.reshape(n_core * R, FH + DC)
    big = [cols[:, :FH], outer_proj[: U // 2], outer_proj[U // 2 :], cols[:, FH:]]
    big = after(jnp.concatenate(big, 1), gate[1], docs)
    big = lax.all_gather(big, CHIP, axis=0, tiled=True)
    w_out_half = big[:, FH + 2 * D :]
    w_out_other = swap(w_out_half, "core", 1)
    by_core = lambda mine, other: jnp.where(
        core == 0, jnp.concatenate([mine, other], 1), jnp.concatenate([other, mine], 1)
    )

    nb = L // BLK
    ends = docs.reshape(M, nb, BLK)
    lo = jnp.sum(docs[:, None, :] < ends[:, :, :1], -1) // 128
    count = (jnp.sum(docs[:, None, :] <= ends[:, :, -1:], -1) - lo * 128 + BLK - 1) // BLK
    lo = jnp.minimum(lo, (L - count * BLK) // 128)
    lohi = jnp.stack([lo, count], -1).reshape(-1).astype(jnp.int32)
    segr = docs.reshape(M, L // 128, 1, 128).astype(F32)
    cos_t, sin_t = rotations(L, half)
    tab = jnp.concatenate([sin_t, sin_t, cos_t, cos_t], 1)
    bias = jnp.stack(
        [heads(full_content).reshape(hl, DH), heads(full_posbias).reshape(hl, DH)], 1
    )
    bias = bias.reshape(pairs, 2, 2 * DH).astype(F32)
    pp = heads(full_posproj).reshape(hl, DH, DH)
    pc, ps = pp[..., :half], pp[..., half:]
    z64 = jnp.zeros((hl, DH, DH), BF)
    mat = jnp.concatenate([z64, pc, -ps, z64, ps, pc], 2)
    mat = jnp.concatenate([jnp.zeros_like(mat), mat], 1).reshape(pairs, 2, 128, 256)
    vb = heads(full_vbias).reshape(pairs, 1, 128).astype(F32)

    qkv = dot(x_all, w_qkv).astype(BF).reshape(M, L, w3)
    ctx, o, lse = attention_forward(qkv, lohi, segr, tab, bias, mat, vb)
    ctx_tok = lax.all_to_all(
        ctx.reshape(M, S, T, width), SEQ, split_axis=1, concat_axis=1, tiled=True
    )
    ctx_tok = ctx_tok.transpose(0, 2, 1, 3).reshape(N, H * DH)
    x_float = x.reshape(N, D).astype(F32)
    attn = by_core(dot(ctx_tok, w_out_half), dot(ctx_tok, w_out_other)) + full_obias
    hidden, first_back = jax.vjp(
        lambda a, g, b: layer_norm(a, g, b), x_float + attn, full_again, full_ashift
    )
    hid = hidden.astype(BF)
    hid2 = swap(hid, "core", 1)
    active, dgelu, part, part_send = ff_forward(hid, hid2, big, full_ibias, FH)
    outer = part + swap(part_send, "core", 1).astype(F32) + full_fbias
    result, second_back = jax.vjp(
        lambda a, g, b: layer_norm(a, g, b), hidden + outer, full_fgain, full_fshift
    )
    output = result.astype(BF).reshape(M, 1, T, D)

    g_hidden, g_fgain, g_fshift = second_back(cotangent[:, 0].reshape(N, D).astype(F32))
    go = g_hidden.astype(BF)
    w_out = by_core(w_out_half, w_out_other)
    go_pair = jnp.concatenate([go, after(swap(go, "core", 1), w_out)], 0)
    FQ = FH // 2
    z_dims = [("dz", b) for b in bits_of("dz")]
    z_bits = z_dims[::-1]
    chip_bits = z_dims + x_bit + yy_bits
    rows = two(chip_bits) + (n_core * R,)
    g_outer_w = [dot(active[:, k * FQ : (k + 1) * FQ], go_pair, 0, 0).astype(BF) for k in range(2)]
    outer_y, outer_x = [Chain([g.reshape(rows + (D,))], chip_bits) for g in g_outer_w]
    outer_y.run(yy_bits[:1])
    outer_x.run(x_bit)
    *g_inner_w, g_ib, g_part, g_send = ff_backward(
        after(go_pair, outer_y.sends[0], outer_x.sends[0]), hid, hid2, big, dgelu, FH
    )
    g_send = meet(g_send, outer_y, outer_x)
    inner_y, inner_x = [
        Chain([g.reshape(rows + (FQ,))], chip_bits) for g in g_inner_w
    ]
    inner_x.run(x_bit)
    inner_y.run(yy_bits[:1])
    g_send = after(g_send, inner_x.sends[0], inner_y.sends[0])
    g_hidden = g_hidden + g_part + swap(g_send, "core", 1).astype(F32)
    g_sum, g_again, g_ashift = first_back(g_hidden)
    ga = g_sum.astype(BF)
    gc = jnp.stack(
        [dot(ga, w_out[k * width : (k + 1) * width], 1, 1).astype(BF) for k in range(S)]
    )
    g_heads = lax.all_to_all(gc, SEQ, split_axis=0, concat_axis=0, tiled=True)
    g_heads = g_heads.reshape(S, M, T, width).transpose(1, 0, 2, 3).reshape(M, L, width)

    ga_cols = after(ga, gc)
    cols = lambda k: lax.dynamic_slice_in_dim(ga_cols, k * DC, DC, 1)
    theirs = swap(dot(ctx_tok, cols(1 - core), 0, 0).astype(BF), "core", 1)
    g_out_half = (dot(ctx_tok, cols(core), 0, 0) + theirs.astype(F32)).astype(BF)
    out_y = Chain([g_out_half.reshape(rows + (DC,))], chip_bits)
    outer_y.terms, outer_x.terms, _ = lax.optimization_barrier((outer_y.terms, outer_x.terms, gc))
    outer_y.run(yy_bits[1:] + x_bit)
    outer_x.run(yy_bits)
    g_heads = meet(after(g_heads, outer_y.sends[-1], outer_x.sends[1]), inner_x, inner_y)
    inner_y.run(yy_bits[1:] + x_bit)
    inner_x.run(yy_bits)
    g_heads = after(g_heads, inner_y.sends[-1], inner_x.sends[1])
    out_y.run(yy_bits)

    gqkv, small = None, []
    for m in range(M):
        gqkv, sm, pp_m = attention_backward(
            m, gqkv, qkv, g_heads, o, lse, lohi, segr, tab, bias, mat
        )
        small.append((sm, pp_m))
        if m == 0:
            gqkv, g_heads = lax.optimization_barrier((gqkv, g_heads))
            g_heads = meet(g_heads, outer_y, outer_x, inner_y, inner_x)
            ff = [outer_y, outer_x, inner_y, inner_x]
            g_heads = after(g_heads, *run_together(ff, z_bits[:1]))
    gqkv = meet(gqkv, out_y, *ff).reshape(M * L, w3)
    run_together(ff, z_bits[1:-1])

    g_qkv_w = dot(x_all, gqkv, 0, 0).astype(BF).reshape(two(z_dims + x_bit) + (S * R, w3))
    mixed = Chain([g_qkv_w], z_dims + x_bit)
    mixed.run(x_bit)
    sent = send_together(ff, z_bits[-1])
    out_y.run(x_bit)
    dx = after(gqkv, mixed.sends[0], sent, out_y.sends[-1])
    dx = dot(dx, w_qkv, 1, 1).astype(BF).reshape((M,) + two(yy_bits) + (2, T, D))
    dx = jnp.moveaxis(dx, 0, len(yy_bits) + 1)
    dx = Chain([dx], yy_bits + [("core", 1)]).run([("core", 1)] + yy_bits)
    colsums = (gc, ga, go, g_again, g_ashift, g_fgain, g_fshift, g_ib)
    (small, colsums, _) = meet((small, colsums, dx.sends[-1]), mixed, out_y)
    mixed.run(z_bits)
    out_y.terms[-1], got, _ = lax.optimization_barrier(
        (out_y.terms[-1], swap(sent, *z_bits[-1]), mixed.sends[-1])
    )
    take_together(ff, got)
    out_y.run(z_bits)
    gc, ga, go, g_again, g_ashift, g_fgain, g_fshift, g_ib = colsums
    gsm, gpp = sum(k[0] for k in small), sum(k[1] for k in small)
    g_mixed = meet(mixed.result().astype(BF), dx)
    g_rows = lax.all_to_all(
        g_mixed.reshape(S, R, 3, width), SEQ, split_axis=0, concat_axis=0, tiled=True
    )
    g_rows = g_rows.astype(F32).transpose(2, 1, 0, 3).reshape(3, R, D)
    input_grad = (g_sum.reshape(M, T, D) + dx.result()).reshape(M, 1, T, D)

    colsum = lambda v: jnp.sum(v.astype(F32), axis=0).reshape(-1)
    gsm = gsm[:, :, :2, :DH].reshape(hl, 2, DH).transpose(1, 0, 2).reshape(2, 1, width)
    here = (jnp.arange(S) == seq).reshape(1, S, 1)
    g_heads_sm = jnp.where(here, gsm, 0.0).reshape(2, D)
    g_rest = [jnp.sum(gc.astype(F32), 1).reshape(-1), colsum(ga)] + [v.reshape(-1) for v in (g_again, g_ashift)]
    g_rest += [colsum(go), g_fgain.reshape(-1), g_fshift.reshape(-1)]
    g_vectors = jnp.concatenate([g_heads_sm, jnp.stack(g_rest)]).astype(BF)
    g_vectors = g_vectors.reshape(n_vec - 1, devices, R).transpose(1, 0, 2)
    g_vectors = jnp.pad(g_vectors, ((0, 0), (0, 0), (0, 128 - R)))
    g_ibias = g_ib.reshape(2, chips, 1, U // 2).transpose(1, 2, 0, 3).reshape(chips, 1, U)
    on_core = (jnp.arange(n_core) == core).reshape(1, n_core, 1)
    g_ibias = jnp.where(on_core, g_ibias, 0.0).reshape(devices, 1, U).astype(BF)
    g_ibias = jnp.pad(g_ibias, ((0, 0), (0, 0), (0, 128 - U)))
    gpp = gpp.reshape(hl, 128, 256)[:, DH:]
    e1, e2 = gpp[:, :, DH : 2 * DH], gpp[:, :, 3 * DH :]
    g_posproj = jnp.concatenate(
        [e1[..., :half] + e2[..., half:], e2[..., :half] - e1[..., half:]], -1
    ).astype(BF)
    g_posproj = jnp.where(here, g_posproj.reshape(1, 1, -1), jnp.zeros((), BF))
    g_posproj = g_posproj.reshape(devices, -1, 128)
    g_packed = jnp.concatenate([g_vectors, g_ibias, g_posproj], 1)
    g_packed = lax.all_to_all(g_packed, ALL, split_axis=0, concat_axis=0, tiled=True)
    g_packed = jnp.sum(g_packed.astype(F32), 0)
    s = [g_packed[k, : v.size] for k, v in enumerate(vectors)]
    g_pp = g_packed[n_vec:].reshape(R, DH)

    outer_grad = jnp.concatenate([outer_y.result(), outer_x.result()], 0)

    def by_rows(v):
        v = v.astype(BF).reshape(n_core, R, -1)
        mine = lax.dynamic_index_in_dim(v, core, 0, False)
        other = swap(lax.dynamic_index_in_dim(v, 1 - core, 0, False), "core", 1)
        return jnp.where(core == 0, mine, other), jnp.where(core == 0, other, mine)

    inner_grad = jnp.stack(by_rows(jnp.concatenate([inner_y.result(), inner_x.result()], 1)), 1)
    inner_grad = inner_grad.reshape(R, n_core, 2, chips, U // 2).transpose(0, 3, 1, 2, 4)
    inner_grad = inner_grad.astype(F32).reshape(R, FF)
    out_grad = jnp.concatenate(by_rows(out_y.result()), 1).astype(F32)

    return (
        output, input_grad, g_rows[0], g_rows[1], g_rows[2], out_grad, s[2], s[0], s[1], g_pp,
        s[3], s[4], s[5], inner_grad, s[9], outer_grad, s[6], s[7], s[8],
    )


def solution(mesh):
    n_dp, n_seq = mesh.devices.shape
    mesh = Mesh(mesh.devices.reshape(n_dp // 2, 2, n_seq // 2, 2), ALL)
    tok, ids = P(None, DP, SEQ, None), P(None, DP, SEQ)
    mat, vec = P(ALL, None), P(ALL)
    in_specs = (
        tok, ids, tok, mat, mat, mat, mat, vec, vec, vec, mat, vec, vec, vec, mat, vec, mat, vec,
        vec, vec,
    )
    out_specs = (
        tok, tok, mat, mat, mat, mat, vec, vec, vec, mat, vec, vec, vec, mat, vec, mat, vec, vec,
        vec,
    )
    return jax.shard_map(
        per_device, mesh=mesh, in_specs=in_specs, out_specs=out_specs, check_vma=False
    )
```

```python
import functools
import math

import jax
import jax.numpy as jnp
from jax import lax
from jax.experimental import pallas as pl
from jax.experimental.pallas import tpu as pltpu
from jax.sharding import Mesh, PartitionSpec as P

H = 16
DH = 64
BLK = 256
GRP = 2
NEG = -1e30
BF = jnp.bfloat16
F32 = jnp.float32
DP = ("dz", "dx")
SEQ = ("yy", "core")
CHIP = DP + ("yy",)
ALL = DP + SEQ


def dot(a, b, ca=1, cb=0):
    return lax.dot_general(a, b, (((ca,), (cb,)), ((), ())), preferred_element_type=F32)


def rotations(length, half_size):
    position = jnp.arange(length, dtype=jnp.int32).astype(F32)
    steps = jnp.arange(half_size, dtype=jnp.int32).astype(F32)
    frequency = jnp.exp(steps * (-math.log(10000.0) / half_size))
    angle = position[:, None] * frequency[None, :]
    return (jnp.cos(angle), jnp.sin(angle))


def layer_norm(values, gain, shift):
    average = jnp.mean(values, axis=-1, keepdims=True)
    centred = values - average
    variance = jnp.mean(centred * centred, axis=-1, keepdims=True)
    return centred * lax.rsqrt(variance + 1e-06) * gain + shift


def gelu_tanh(values):
    return jax.nn.gelu(values, approximate=True)


def swap(x, axis, bit):
    n = lax.axis_size(axis)
    return lax.ppermute(x, axis, [(i, i ^ bit) for i in range(n)])


def side(axis, bit):
    return jnp.where((lax.axis_index(axis) & bit) != 0, 1, 0)


def double(x, axis, bit, dim, other=None):
    other = swap(x, axis, bit) if other is None else other
    mine = side(axis, bit) == 0
    return jnp.stack([jnp.where(mine, x, other), jnp.where(mine, other, x)], dim)


def bits_of(axis):
    n = lax.axis_size(axis)
    return [1 << k for k in reversed(range(n.bit_length() - 1))]


def gather_bits(x, axis, dim=0, wait=None):
    bits = bits_of(axis)
    for k, bit in enumerate(bits):
        x = double(x, axis, bit, dim + k)
        if wait is not None and k == 0:
            behind = tuple(wait)
            wait.append(x)
            x = after(x, *behind)
    return x.reshape(x.shape[:dim] + (lax.axis_size(axis),) + x.shape[dim + len(bits) :])


def total(terms):
    return sum(t.astype(F32) for t in terms)


class Chain:
    def __init__(self, terms, left):
        self.terms, self.left, self.sends = terms, list(left), []

    def send(self, step):
        axis, bit = step
        dim = self.left.index(step)
        self.left.pop(dim)
        mine = side(axis, bit)
        take = lambda t, k: lax.dynamic_index_in_dim(t, k, dim, keepdims=False)
        out = total([take(t, 1 - mine) for t in self.terms]).astype(BF)
        self.terms = [take(t, mine) for t in self.terms]
        self.sends.append(out)
        return out

    def run(self, steps):
        for step in steps:
            got = swap(self.send(step), *step)
            self.terms.append(got)
        return self

    def result(self):
        return total(self.terms)


def send_together(chains, step):
    return jnp.concatenate([c.send(step) for c in chains], -1)


def take_together(chains, got):
    at = 0
    for c in chains:
        width = c.terms[0].shape[-1]
        c.terms.append(got[..., at : at + width])
        at += width


def run_together(chains, steps):
    sends = []
    for step in steps:
        sends.append(send_together(chains, step))
        take_together(chains, swap(sends[-1], *step))
    return sends


def after(x, *others):
    return lax.optimization_barrier((x,) + others)[0]


def meet(x, *chains):
    x, last = lax.optimization_barrier((x, [c.terms[-1] for c in chains]))
    for c, t in zip(chains, last):
        c.terms[-1] = t
    return x


def tables(tab):
    lane = lax.broadcasted_iota(jnp.int32, tab.shape, 1)
    turned = pltpu.roll(tab, DH, 1)
    cos = jnp.where(lane < DH, 0.0, tab)
    sin = jnp.where(lane < DH, 0.0, turned)
    return cos, sin, jnp.where(lane < DH + DH // 2, tab, turned)


def prep_head(e, q, qr, k, kr, first, bias, mat, cos, sin, pk):
    base = jnp.where(first, q, qr) if e == 0 else jnp.where(first, qr, q)
    both = (base + bias).astype(BF)
    turned = dot(both, mat)
    rel = turned[:, :128] * cos + turned[:, 128:] * sin
    qf = (jnp.where(first, both.astype(F32), rel) * (DH**-0.5)).astype(BF)
    kf = jnp.where(first, k if e == 0 else kr, pk).astype(BF)
    return both, qf, kf


def row_of(ref, start, width):
    return jnp.concatenate([ref[0, start + t] for t in range(width // 128)], 1)


def seg_columns(segr_ref, seg_s, i):
    for t in range(i * (BLK // 128), (i + 1) * (BLK // 128)):
        tile = jnp.broadcast_to(segr_ref[0, t], (128, 128)).T
        seg_s[t * 128 : (t + 1) * 128, :] = tile


def by_width(n, most, body):
    for k in range(1, most + 1):

        @pl.when(n == k)
        def _(k=k):
            body(k * BLK)


def fwd_kernel(
    lohi, q_ref, k_ref, v_ref, segr_ref, tab_ref, bias_ref, mat_ref, vb_ref,
    ctx_ref, o_ref, lse_ref, qf_s, kf_s, seg_s,
):
    m = pl.program_id(0)
    nb = q_ref.shape[1] // BLK
    first = lax.broadcasted_iota(jnp.int32, (BLK, 128), 1) < DH

    def prep(i):
        rows = slice(i * BLK, (i + 1) * BLK)
        seg_columns(segr_ref, seg_s, i)
        q = q_ref[0, rows, :].astype(F32)
        k = k_ref[0, rows, :].astype(F32)
        qr, kr = pltpu.roll(q, DH, 1), pltpu.roll(k, DH, 1)
        cos, sin, pk = tables(tab_ref[rows, :])
        for e in range(2):
            _, qf, kf = prep_head(
                e, q, qr, k, kr, first, bias_ref[0, e : e + 1, :], mat_ref[0, e],
                cos, sin, pk,
            )
            qf_s[e, rows, :] = qf
            kf_s[e, rows, :] = kf

    for i in range(nb):
        prep(i)

    def q_group(i, c):
        at = (m * nb + i * GRP) * 2
        starts = [lohi[at + 2 * u] for u in range(GRP)]
        n = lohi[at + 1]
        for u in range(1, GRP):
            n = jnp.maximum(n, lohi[at + 2 * u + 1])

        def body(width):
            for u in range(GRP):
                rows = pl.ds(pl.multiple_of((i * GRP + u) * BLK, BLK), BLK)
                start = jnp.minimum(starts[u], (nb * BLK - width) // 128)
                cols = pl.ds(pl.multiple_of(start * 128, 128), width)
                segq = jnp.concatenate([seg_s[rows, :]] * (width // 128), 1)
                same = segq == row_of(segr_ref, start, width)
                outs = []
                for e in range(2):
                    s = dot(qf_s[e, rows, :], kf_s[e, cols, :], 1, 1)
                    s = jnp.where(same, s, NEG)
                    top = jnp.max(s, axis=1, keepdims=True)
                    p = jnp.exp(s - top)
                    total = jnp.sum(p, axis=1, keepdims=True)
                    acc = dot(p.astype(BF), v_ref[0, cols, :])
                    outs.append((acc / total, top + jnp.log(total)))
                o = jnp.where(first, outs[0][0], outs[1][0])
                o_ref[0, rows, :] = o.astype(BF)
                lse_t = jnp.where(first, outs[0][1], outs[1][1]).T
                for e in range(2):
                    for t in range(BLK // 128):
                        lse_ref[0, 0, e, (i * GRP + u) * (BLK // 128) + t] = lse_t[
                            e * DH : e * DH + 1, t * 128 : t * 128 + 128
                        ]
                ctx_ref[0, rows, :] = (o + vb_ref[0]).astype(BF)

        by_width(n, nb, body)
        return c

    lax.fori_loop(0, nb // GRP, q_group, 0)


def bwd_kernel(
    m, lohi, q_ref, k_ref, v_ref, g_ref, o_ref, lse_ref, segr_ref, tab_ref, bias_ref,
    mat_ref, *refs,
):
    gqkv_ref, gsm_ref, gpp_ref, both_s, qf_s, kf_s, seg_s, dl_s, gq_s, res_s = refs[-10:]
    p = pl.program_id(0)
    nb = q_ref.shape[1] // BLK
    width3 = gqkv_ref.shape[2] // 3
    first = lax.broadcasted_iota(jnp.int32, (BLK, 128), 1) < DH

    def prep(i):
        rows = slice(i * BLK, (i + 1) * BLK)
        seg_columns(segr_ref, seg_s, i)
        q = q_ref[0, rows, :].astype(F32)
        k = k_ref[0, rows, :].astype(F32)
        qr, kr = pltpu.roll(q, DH, 1), pltpu.roll(k, DH, 1)
        cos, sin, pk = tables(tab_ref[rows, :])
        dl_t = (g_ref[0, rows, :].astype(F32) * o_ref[0, rows, :].astype(F32)).T
        for e in range(2):
            both, qf, kf = prep_head(
                e, q, qr, k, kr, first, bias_ref[0, e : e + 1, :], mat_ref[0, e],
                cos, sin, pk,
            )
            both_s[e, rows, :] = both
            qf_s[e, rows, :] = qf
            kf_s[e, rows, :] = kf
            gq_s[e, rows, :] = jnp.zeros((BLK, 128), F32)
            dl = jnp.sum(dl_t[e * DH : (e + 1) * DH, :], axis=0, keepdims=True)
            for t in range(BLK // 128):
                dl_s[e, i * (BLK // 128) + t] = dl[:, t * 128 : t * 128 + 128]

    for i in range(nb):
        prep(i)

    def k_group(j, c):
        at = (m * nb + j * GRP) * 2
        starts = [lohi[at + 2 * u] for u in range(GRP)]
        n = lohi[at + 1]
        for u in range(1, GRP):
            n = jnp.maximum(n, lohi[at + 2 * u + 1])

        def body(width):
            for u in range(GRP):
                rows = pl.ds(pl.multiple_of((j * GRP + u) * BLK, BLK), BLK)
                start = jnp.minimum(starts[u], (nb * BLK - width) // 128)
                cols = pl.ds(pl.multiple_of(start * 128, 128), width)
                segk = jnp.concatenate([seg_s[rows, :]] * (width // 128), 1)
                same = segk == row_of(segr_ref, start, width)
                g = g_ref[0, cols, :]
                v = v_ref[0, rows, :].astype(F32)
                outs = []
                for e in range(2):
                    row = lambda ref: jnp.concatenate(
                        [ref[e, start + t] for t in range(width // 128)], 1
                    )
                    mine = first if e == 0 else jnp.logical_not(first)
                    vm = jnp.where(mine, v, 0.0).astype(BF)
                    kf, qf = kf_s[e, rows, :], qf_s[e, cols, :]
                    prob = jnp.where(same, jnp.exp(dot(kf, qf, 1, 1) - row(lse_ref.at[0, 0])), 0.0)
                    ds = (prob * (dot(vm, g, 1, 1) - row(dl_s))).astype(BF)
                    gv = dot(prob.astype(BF), g)
                    gk = dot(ds, qf)
                    gq_s[e, cols, :] = gq_s[e, cols, :] + dot(ds, kf, 0, 0)
                    outs.append((gk, gv))
                res_s[1, rows, :] = jnp.where(first, outs[0][0], pltpu.roll(outs[1][0], DH, 1))
                res_s[2, rows, :] = jnp.where(first, outs[0][1], outs[1][1])

        by_width(n, nb, body)
        return c

    lax.fori_loop(0, nb // GRP, k_group, 0)

    def finish(i, carry):
        rows = pl.ds(pl.multiple_of(i * BLK, BLK), BLK)
        new, gqs = [], []
        cos, sin, _ = tables(tab_ref[rows, :])
        for e in range(2):
            s_content, s_pos, s_proj = carry[e]
            g = gq_s[e, rows, :] * (DH**-0.5)
            turned = jnp.concatenate(
                [(g * cos).astype(BF), (g * sin).astype(BF)], 1
            )
            swapped = jnp.concatenate([mat_ref[0, e, DH:, :], mat_ref[0, e, :DH, :]], 0)
            gqp = dot(turned, swapped, 1, 1)
            gqs.append(g + gqp)
            s_content = s_content + jnp.sum(g, axis=0, keepdims=True)
            s_pos = s_pos + jnp.sum(gqp, axis=0, keepdims=True)
            s_proj = s_proj + dot(both_s[e, rows, :], turned, 0, 0)
            new.append((s_content, s_pos, s_proj))
        res_s[0, rows, :] = jnp.where(first, gqs[0], pltpu.roll(gqs[1], DH, 1))
        return tuple(new)

    row0 = jnp.zeros((1, 128), F32)
    zero = (row0, row0, jnp.zeros((128, 256), F32))
    sums = lax.fori_loop(0, nb, finish, (zero, zero), unroll=True)
    for e in range(2):
        gsm_ref[0, e, 0:1, :] = sums[e][0]
        gsm_ref[0, e, 1:2, :] = sums[e][1]
        gpp_ref[0, e] = sums[e][2]

    for at in range(width3 // 128):

        @pl.when(p == at)
        def _(at=at):
            for part in range(3):
                off = part * width3 + at * 128
                gqkv_ref[0, :, off : off + 128] = res_s[part].astype(BF)


def attention_specs(L, width):
    pairs = width // 128
    pair = lambda k: pl.BlockSpec((1, L, 128), lambda m, p, *_: (m, 0, k * pairs + p))
    per_m = lambda *s: pl.BlockSpec((1,) + s, lambda m, p, *_: (m,) + (0,) * len(s))
    per_p = lambda *s: pl.BlockSpec((1,) + s, lambda m, p, *_: (p,) + (0,) * len(s))
    whole = lambda *s: pl.BlockSpec(s, lambda m, p, *_: (0,) * len(s))
    return pairs, pair, per_m, per_p, whole


def attention_forward(qkv, lohi, segr, tab, bias, mat, vb):
    M, L, w3 = qkv.shape
    width = w3 // 3
    nb = L // BLK
    pairs, pair, per_m, per_p, whole = attention_specs(L, width)
    return pl.pallas_call(
        fwd_kernel,
        out_shape=(
            jax.ShapeDtypeStruct((M, L, width), BF),
            jax.ShapeDtypeStruct((M, L, width), BF),
            jax.ShapeDtypeStruct((M, pairs, 2, L // 128, 1, 128), F32),
        ),
        grid_spec=pltpu.PrefetchScalarGridSpec(
            num_scalar_prefetch=1,
            grid=(M, pairs),
            in_specs=[
                pair(0), pair(1), pair(2), per_m(L // 128, 1, 128), whole(L, 128), per_p(2, 128),
                per_p(2, 128, 256), per_p(1, 128),
            ],
            out_specs=[
                pair(0), pair(0),
                pl.BlockSpec((1, 1, 2, L // 128, 1, 128), lambda m, p, *_: (m, p, 0, 0, 0, 0)),
            ],
            scratch_shapes=[
                pltpu.VMEM((2, L, 128), BF),
                pltpu.VMEM((2, L, 128), BF),
                pltpu.VMEM((L, 128), F32),
            ],
        ),
        compiler_params=pltpu.CompilerParams(
            dimension_semantics=("arbitrary", "arbitrary"), vmem_limit_bytes=32 << 20
        ),
        name="attend",
    )(lohi, qkv, qkv, qkv, segr, tab, bias, mat, vb)


def attention_backward(m, into, qkv, g, o, lse, lohi, segr, tab, bias, mat):
    M, L, w3 = qkv.shape
    more = [] if into is None else [into]
    width = w3 // 3
    pairs = width // 128
    pair = lambda k: pl.BlockSpec((1, L, 128), lambda p, *_: (m, 0, k * pairs + p))
    per_m = lambda *s: pl.BlockSpec((1,) + s, lambda p, *_: (m,) + (0,) * len(s))
    per_p = lambda *s: pl.BlockSpec((1,) + s, lambda p, *_: (p,) + (0,) * len(s))
    whole = lambda *s: pl.BlockSpec(s, lambda p, *_: (0,) * len(s))
    return pl.pallas_call(
        functools.partial(bwd_kernel, m),
        out_shape=(
            jax.ShapeDtypeStruct((M, L, w3), BF),
            jax.ShapeDtypeStruct((pairs, 2, 8, 128), F32),
            jax.ShapeDtypeStruct((pairs, 2, 128, 256), F32),
        ),
        grid_spec=pltpu.PrefetchScalarGridSpec(
            num_scalar_prefetch=1,
            grid=(pairs,),
            in_specs=[
                pair(0), pair(1), pair(2), pair(0), pair(0),
                pl.BlockSpec((1, 1, 2, L // 128, 1, 128), lambda p, *_: (m, p, 0, 0, 0, 0)),
                per_m(L // 128, 1, 128),
                whole(L, 128), per_p(2, 128), per_p(2, 128, 256),
            ] + [pl.BlockSpec(memory_space=pl.ANY) for _ in more],
            out_specs=[per_m(L, w3), per_p(2, 8, 128), per_p(2, 128, 256)],
            scratch_shapes=[
                pltpu.VMEM((2, L, 128), BF),
                pltpu.VMEM((2, L, 128), BF),
                pltpu.VMEM((2, L, 128), BF),
                pltpu.VMEM((L, 128), F32),
                pltpu.VMEM((2, L // 128, 1, 128), F32),
                pltpu.VMEM((2, L, 128), F32),
                pltpu.VMEM((3, L, 128), F32),
            ],
        ),
        compiler_params=pltpu.CompilerParams(
            dimension_semantics=("arbitrary",), vmem_limit_bytes=46 << 20
        ),
        input_output_aliases={11: 0} if more else {},
        name="attend_back",
    )(lohi, qkv, qkv, qkv, g, o, lse, segr, tab, bias, mat, *more)


UB = 512


def ff_forward_kernel(
    hid_ref, hid2_ref, wi_ref, wo_ref, ib_ref, act_ref, dg_ref, own_ref, send_ref, acc
):
    u = pl.program_id(0)
    n2 = 2 * hid_ref.shape[0]
    RB = n2 // 2
    for r in range(n2 // RB):
        rows = slice(r * RB, (r + 1) * RB)
        v = dot((hid_ref if r == 0 else hid2_ref)[...], wi_ref[...]) + ib_ref[...]
        c = math.sqrt(2.0 / math.pi)
        v2 = v * v
        t = jnp.tanh(c * v * (1.0 + 0.044715 * v2))
        h = 0.5 * (1.0 + t)
        act = (v * h).astype(BF)
        dg = h + (0.5 * c) * v * (1.0 - t * t) * (1.0 + (3 * 0.044715) * v2)
        act_ref[rows, :] = act
        dg_ref[rows, :] = dg.astype(BF)
        new = dot(act, wo_ref[...])

        @pl.when(u == 0)
        def _(rows=rows, new=new):
            acc[rows, :] = new

        @pl.when(u > 0)
        def _(rows=rows, new=new):
            acc[rows, :] = acc[rows, :] + new

    @pl.when(u == pl.num_programs(0) - 1)
    def _():
        own_ref[...] = acc[: n2 // 2, :]
        send_ref[...] = acc[n2 // 2 :, :].astype(BF)


def ff_backward_kernel(
    go_ref, hid_ref, hid2_ref, wi_ref, wo_ref, dg_ref, ga_ref, gb_ref, gib_ref, own_ref,
    send_ref, acc, hid_t, gi_s,
):
    u = pl.program_id(0)
    n2 = go_ref.shape[0]
    RB = n2 // 2

    @pl.when(u == 0)
    def _():
        hid_t[:, : n2 // 2] = hid_ref[...].T
        hid_t[:, n2 // 2 :] = hid2_ref[...].T

    total = jnp.zeros((1, UB), F32)
    for r in range(n2 // RB):
        rows = slice(r * RB, (r + 1) * RB)
        gi = (dot(go_ref[rows, :], wo_ref[...], 1, 1) * dg_ref[rows, :].astype(F32)).astype(BF)
        gi_s[rows, :] = gi
        total = total + jnp.sum(gi.astype(F32), axis=0, keepdims=True)
        new = dot(gi, wi_ref[...], 1, 1)

        @pl.when(u == 0)
        def _(rows=rows, new=new):
            acc[rows, :] = new

        @pl.when(u > 0)
        def _(rows=rows, new=new):
            acc[rows, :] = acc[rows, :] + new

    gib_ref[...] = total
    g = dot(hid_t[...], gi_s[...]).astype(BF)

    @pl.when(u < pl.num_programs(0) // 2)
    def _():
        ga_ref[...] = g

    @pl.when(u >= pl.num_programs(0) // 2)
    def _():
        gb_ref[...] = g

    @pl.when(u == pl.num_programs(0) - 1)
    def _():
        own_ref[...] = acc[: n2 // 2, :]
        send_ref[...] = acc[n2 // 2 :, :].astype(BF)


def ff_specs(n2, d, fh):
    nq = fh // 2 // UB
    fixed = lambda *shape: pl.BlockSpec(shape, lambda u: (0,) * len(shape))
    units = lambda rows: pl.BlockSpec((rows, UB), lambda u: (0, u))
    outer = pl.BlockSpec((UB, d), lambda u: (lax.rem(u, nq), fh // d + u // nq))
    return fixed, units, outer


def ff_forward(hid, hid2, big, ib, fh):
    n2, d = 2 * hid.shape[0], hid.shape[1]
    fixed, units, outer = ff_specs(n2, d, fh)
    return pl.pallas_call(
        ff_forward_kernel,
        out_shape=(
            jax.ShapeDtypeStruct((n2, fh), BF),
            jax.ShapeDtypeStruct((n2, fh), BF),
            jax.ShapeDtypeStruct((n2 // 2, d), F32),
            jax.ShapeDtypeStruct((n2 // 2, d), BF),
        ),
        grid=(fh // UB,),
        in_specs=[fixed(n2 // 2, d), fixed(n2 // 2, d), units(d), outer, units(1)],
        out_specs=[units(n2), units(n2), fixed(n2 // 2, d), fixed(n2 // 2, d)],
        scratch_shapes=[pltpu.VMEM((n2, d), F32)],
        compiler_params=pltpu.CompilerParams(
            dimension_semantics=("arbitrary",), vmem_limit_bytes=56 << 20
        ),
        name="feed",
    )(hid, hid2, big, big, ib)


def ff_backward(go, hid, hid2, big, dg, fh):
    n2, d = go.shape
    fixed, units, outer = ff_specs(n2, d, fh)
    nq = fh // 2 // UB
    return pl.pallas_call(
        ff_backward_kernel,
        out_shape=(
            jax.ShapeDtypeStruct((d, fh // 2), BF),
            jax.ShapeDtypeStruct((d, fh // 2), BF),
            jax.ShapeDtypeStruct((1, fh), F32),
            jax.ShapeDtypeStruct((n2 // 2, d), F32),
            jax.ShapeDtypeStruct((n2 // 2, d), BF),
        ),
        grid=(fh // UB,),
        in_specs=[
            fixed(n2, d), fixed(n2 // 2, d), fixed(n2 // 2, d), units(d), outer, units(n2),
        ],
        out_specs=[
            pl.BlockSpec((d, UB), lambda u: (0, jnp.minimum(u, nq - 1))),
            pl.BlockSpec((d, UB), lambda u: (0, jnp.maximum(u - nq, 0))),
            units(1), fixed(n2 // 2, d), fixed(n2 // 2, d),
        ],
        scratch_shapes=[
            pltpu.VMEM((n2, d), F32),
            pltpu.VMEM((d, n2), BF),
            pltpu.VMEM((n2, UB), BF),
        ],
        compiler_params=pltpu.CompilerParams(
            dimension_semantics=("arbitrary",), vmem_limit_bytes=44 << 20
        ),
        name="feed_back",
    )(go, hid, hid2, big, big, dg)


def per_device(
    tokens, segment_ids, cotangent, query_proj, key_proj, value_proj, out_proj, value_bias,
    content_bias, position_bias, position_proj, out_bias, attn_gain, attn_shift, inner_proj,
    inner_bias, outer_proj, outer_bias, final_gain, final_shift,
):
    M, _, T, D = tokens.shape
    n_dz, n_dx, n_yy, n_core = (lax.axis_size(a) for a in ALL)
    S = n_yy * n_core
    chips = n_dz * n_dx * n_yy
    devices = chips * n_core
    L = T * S
    R = query_proj.shape[0]
    U = outer_proj.shape[0]
    FF = U * devices
    hl = H // S
    width = hl * DH
    pairs = width // 128
    half = DH // 2
    N = M * T
    core = lax.axis_index("core")
    seq = lax.axis_index("yy") * n_core + core
    x_bit = [("dx", 1)]
    yy_bits = [("yy", b) for b in bits_of("yy")]
    two = lambda bits: (2,) * len(bits)

    x = tokens[:, 0]
    x_other = swap(x, "yy", yy_bits[0][1])
    docs = lax.all_gather(segment_ids[:, 0], SEQ, axis=1, tiled=True)
    gate = [x_other]
    by_seq = jnp.stack([query_proj, key_proj, value_proj], 0).reshape(3, R, S, width)
    w3 = 3 * width
    by_seq = by_seq.transpose(2, 1, 0, 3).reshape(S, R, w3)
    mixed = lax.all_to_all(by_seq, SEQ, split_axis=0, concat_axis=0, tiled=True)
    z_first = gather_bits(gather_bits(mixed[..., : w3 // 2], "dz", 0, gate), "dx", 1)
    x_first = gather_bits(gather_bits(mixed[..., w3 // 2 :], "dx"), "dz")
    w_qkv = jnp.concatenate([z_first, x_first], -1).reshape(D, w3)

    row = lambda v: jnp.pad(v, (0, 128 - v.size))
    vectors = [
        content_bias, position_bias, value_bias, out_bias, attn_gain, attn_shift, outer_bias,
        final_gain, final_shift, inner_bias,
    ]
    n_vec = len(vectors)
    packed = jnp.concatenate([jnp.stack([row(v) for v in vectors]), position_proj.reshape(-1, 128)])
    n_pack = packed.shape[0]
    packed = jnp.broadcast_to(after(packed, gate[1])[None], (devices, n_pack, 128))
    packed = lax.all_to_all(packed, ALL, split_axis=0, concat_axis=0, tiled=True)
    heads = lambda v: lax.dynamic_slice_in_dim(v.reshape(S, -1), seq, 1, 0)
    full = [packed[:, k, :R] for k in range(n_vec - 1)]
    full_content, full_posbias, full_vbias = full[:3]
    full_posproj = packed[:, n_vec:].reshape(devices, -1)
    vec = lambda v: v.reshape(1, -1).astype(F32)
    full_obias, full_again, full_ashift, full_fbias, full_fgain, full_fshift = map(vec, full[3:9])
    ib = packed[:, n_vec - 1, :U].reshape(chips, n_core, 2, U // 2)
    ib = lax.dynamic_index_in_dim(ib, core, 1, False)
    full_ibias = ib.transpose(1, 0, 2).reshape(1, -1).astype(F32)

    x_all = x
    for k, (axis, bit) in enumerate(yy_bits):
        x_all = double(x_all, axis, bit, 1 + k, x_other if k == 0 else None)
    x_all = x_all.reshape(M, n_yy, T, D)
    x_all = double(x_all, "core", 1, 2).reshape(M * L, D)

    FH, DC = FF // n_core, D // n_core
    inner_cols = inner_proj.reshape(R, chips, n_core, 2, U // 2).transpose(2, 0, 3, 1, 4)
    out_cols = out_proj.reshape(R, n_core, DC).transpose(1, 0, 2)
    cols = jnp.concatenate([inner_cols.reshape(n_core, R, FH), out_cols], 2)
    cols = lax.all_to_all(cols, "core", split_axis=0, concat_axis=0, tiled=True)
    cols = cols.reshape(n_core * R, FH + DC)
    big = [cols[:, :FH], outer_proj[: U // 2], outer_proj[U // 2 :], cols[:, FH:]]
    big = after(jnp.concatenate(big, 1), gate[1], docs)
    big = lax.all_gather(big, CHIP, axis=0, tiled=True)
    w_out_half = big[:, FH + 2 * D :]
    w_out_other = swap(w_out_half, "core", 1)
    by_core = lambda mine, other: jnp.where(
        core == 0, jnp.concatenate([mine, other], 1), jnp.concatenate([other, mine], 1)
    )

    nb = L // BLK
    ends = docs.reshape(M, nb, BLK)
    lo = jnp.sum(docs[:, None, :] < ends[:, :, :1], -1) // 128
    count = (jnp.sum(docs[:, None, :] <= ends[:, :, -1:], -1) - lo * 128 + BLK - 1) // BLK
    lo = jnp.minimum(lo, (L - count * BLK) // 128)
    lohi = jnp.stack([lo, count], -1).reshape(-1).astype(jnp.int32)
    segr = docs.reshape(M, L // 128, 1, 128).astype(F32)
    cos_t, sin_t = rotations(L, half)
    tab = jnp.concatenate([sin_t, sin_t, cos_t, cos_t], 1)
    bias = jnp.stack(
        [heads(full_content).reshape(hl, DH), heads(full_posbias).reshape(hl, DH)], 1
    )
    bias = bias.reshape(pairs, 2, 2 * DH).astype(F32)
    pp = heads(full_posproj).reshape(hl, DH, DH)
    pc, ps = pp[..., :half], pp[..., half:]
    z64 = jnp.zeros((hl, DH, DH), BF)
    mat = jnp.concatenate([z64, pc, -ps, z64, ps, pc], 2)
    mat = jnp.concatenate([jnp.zeros_like(mat), mat], 1).reshape(pairs, 2, 128, 256)
    vb = heads(full_vbias).reshape(pairs, 1, 128).astype(F32)

    qkv = dot(x_all, w_qkv).astype(BF).reshape(M, L, w3)
    ctx, o, lse = attention_forward(qkv, lohi, segr, tab, bias, mat, vb)
    ctx_tok = lax.all_to_all(
        ctx.reshape(M, S, T, width), SEQ, split_axis=1, concat_axis=1, tiled=True
    )
    ctx_tok = ctx_tok.transpose(0, 2, 1, 3).reshape(N, H * DH)
    x_float = x.reshape(N, D).astype(F32)
    attn = by_core(dot(ctx_tok, w_out_half), dot(ctx_tok, w_out_other)) + full_obias
    hidden, first_back = jax.vjp(
        lambda a, g, b: layer_norm(a, g, b), x_float + attn, full_again, full_ashift
    )
    hid = hidden.astype(BF)
    hid2 = swap(hid, "core", 1)
    active, dgelu, part, part_send = ff_forward(hid, hid2, big, full_ibias, FH)
    outer = part + swap(part_send, "core", 1).astype(F32) + full_fbias
    result, second_back = jax.vjp(
        lambda a, g, b: layer_norm(a, g, b), hidden + outer, full_fgain, full_fshift
    )
    output = result.astype(BF).reshape(M, 1, T, D)

    g_hidden, g_fgain, g_fshift = second_back(cotangent[:, 0].reshape(N, D).astype(F32))
    go = g_hidden.astype(BF)
    w_out = by_core(w_out_half, w_out_other)
    go_pair = jnp.concatenate([go, after(swap(go, "core", 1), w_out)], 0)
    FQ = FH // 2
    z_dims = [("dz", b) for b in bits_of("dz")]
    z_bits = z_dims[::-1]
    chip_bits = z_dims + x_bit + yy_bits
    rows = two(chip_bits) + (n_core * R,)
    g_outer_w = [dot(active[:, k * FQ : (k + 1) * FQ], go_pair, 0, 0).astype(BF) for k in range(2)]
    outer_y, outer_x = [Chain([g.reshape(rows + (D,))], chip_bits) for g in g_outer_w]
    outer_y.run(yy_bits[:1])
    outer_x.run(x_bit)
    *g_inner_w, g_ib, g_part, g_send = ff_backward(
        after(go_pair, outer_y.sends[0], outer_x.sends[0]), hid, hid2, big, dgelu, FH
    )
    g_send = meet(g_send, outer_y, outer_x)
    inner_y, inner_x = [
        Chain([g.reshape(rows + (FQ,))], chip_bits) for g in g_inner_w
    ]
    inner_x.run(x_bit)
    inner_y.run(yy_bits[:1])
    g_send = after(g_send, inner_x.sends[0], inner_y.sends[0])
    g_hidden = g_hidden + g_part + swap(g_send, "core", 1).astype(F32)
    g_sum, g_again, g_ashift = first_back(g_hidden)
    ga = g_sum.astype(BF)
    gc = jnp.stack(
        [dot(ga, w_out[k * width : (k + 1) * width], 1, 1).astype(BF) for k in range(S)]
    )
    g_heads = lax.all_to_all(gc, SEQ, split_axis=0, concat_axis=0, tiled=True)
    g_heads = g_heads.reshape(S, M, T, width).transpose(1, 0, 2, 3).reshape(M, L, width)

    ga_cols = after(ga, gc)
    cols = lambda k: lax.dynamic_slice_in_dim(ga_cols, k * DC, DC, 1)
    theirs = swap(dot(ctx_tok, cols(1 - core), 0, 0).astype(BF), "core", 1)
    g_out_half = (dot(ctx_tok, cols(core), 0, 0) + theirs.astype(F32)).astype(BF)
    out_y = Chain([g_out_half.reshape(rows + (DC,))], chip_bits)
    outer_y.terms, outer_x.terms, _ = lax.optimization_barrier((outer_y.terms, outer_x.terms, gc))
    outer_y.run(yy_bits[1:] + x_bit)
    outer_x.run(yy_bits)
    g_heads = meet(after(g_heads, outer_y.sends[-1], outer_x.sends[1]), inner_x, inner_y)
    inner_y.run(yy_bits[1:] + x_bit)
    inner_x.run(yy_bits)
    g_heads = after(g_heads, inner_y.sends[-1], inner_x.sends[1])
    out_y.run(yy_bits)

    gqkv, small = None, []
    for m in range(M):
        gqkv, sm, pp_m = attention_backward(
            m, gqkv, qkv, g_heads, o, lse, lohi, segr, tab, bias, mat
        )
        small.append((sm, pp_m))
        if m == 0:
            gqkv, g_heads = lax.optimization_barrier((gqkv, g_heads))
            g_heads = meet(g_heads, outer_y, outer_x, inner_y, inner_x)
            ff = [outer_y, outer_x, inner_y, inner_x]
            g_heads = after(g_heads, *run_together(ff, z_bits[:1]))
    gqkv = meet(gqkv, out_y, *ff).reshape(M * L, w3)
    run_together(ff, z_bits[1:-1])

    g_qkv_w = dot(x_all, gqkv, 0, 0).astype(BF).reshape(two(z_dims + x_bit) + (S * R, w3))
    mixed = Chain([g_qkv_w], z_dims + x_bit)
    mixed.run(x_bit)
    sent = send_together(ff, z_bits[-1])
    out_y.run(x_bit)
    dx = after(gqkv, mixed.sends[0], sent, out_y.sends[-1])
    dx = dot(dx, w_qkv, 1, 1).astype(BF).reshape((M,) + two(yy_bits) + (2, T, D))
    dx = jnp.moveaxis(dx, 0, len(yy_bits) + 1)
    dx = Chain([dx], yy_bits + [("core", 1)]).run([("core", 1)] + yy_bits)
    colsums = (gc, ga, go, g_again, g_ashift, g_fgain, g_fshift, g_ib)
    (small, colsums, _) = meet((small, colsums, dx.sends[-1]), mixed, out_y)
    mixed.run(z_bits)
    out_y.terms[-1], got, _ = lax.optimization_barrier(
        (out_y.terms[-1], swap(sent, *z_bits[-1]), mixed.sends[-1])
    )
    take_together(ff, got)
    out_y.run(z_bits)
    gc, ga, go, g_again, g_ashift, g_fgain, g_fshift, g_ib = colsums
    gsm, gpp = sum(k[0] for k in small), sum(k[1] for k in small)
    g_mixed = meet(mixed.result().astype(BF), dx)
    g_rows = lax.all_to_all(
        g_mixed.reshape(S, R, 3, width), SEQ, split_axis=0, concat_axis=0, tiled=True
    )
    g_rows = g_rows.astype(F32).transpose(2, 1, 0, 3).reshape(3, R, D)
    input_grad = (g_sum.reshape(M, T, D) + dx.result()).reshape(M, 1, T, D)

    colsum = lambda v: jnp.sum(v.astype(F32), axis=0).reshape(-1)
    gsm = gsm[:, :, :2, :DH].reshape(hl, 2, DH).transpose(1, 0, 2).reshape(2, 1, width)
    here = (jnp.arange(S) == seq).reshape(1, S, 1)
    g_heads_sm = jnp.where(here, gsm, 0.0).reshape(2, D)
    g_rest = [jnp.sum(gc.astype(F32), 1).reshape(-1), colsum(ga)] + [v.reshape(-1) for v in (g_again, g_ashift)]
    g_rest += [colsum(go), g_fgain.reshape(-1), g_fshift.reshape(-1)]
    g_vectors = jnp.concatenate([g_heads_sm, jnp.stack(g_rest)]).astype(BF)
    g_vectors = g_vectors.reshape(n_vec - 1, devices, R).transpose(1, 0, 2)
    g_vectors = jnp.pad(g_vectors, ((0, 0), (0, 0), (0, 128 - R)))
    g_ibias = g_ib.reshape(2, chips, 1, U // 2).transpose(1, 2, 0, 3).reshape(chips, 1, U)
    on_core = (jnp.arange(n_core) == core).reshape(1, n_core, 1)
    g_ibias = jnp.where(on_core, g_ibias, 0.0).reshape(devices, 1, U).astype(BF)
    g_ibias = jnp.pad(g_ibias, ((0, 0), (0, 0), (0, 128 - U)))
    gpp = gpp.reshape(hl, 128, 256)[:, DH:]
    e1, e2 = gpp[:, :, DH : 2 * DH], gpp[:, :, 3 * DH :]
    g_posproj = jnp.concatenate(
        [e1[..., :half] + e2[..., half:], e2[..., :half] - e1[..., half:]], -1
    ).astype(BF)
    g_posproj = jnp.where(here, g_posproj.reshape(1, 1, -1), jnp.zeros((), BF))
    g_posproj = g_posproj.reshape(devices, -1, 128)
    g_packed = jnp.concatenate([g_vectors, g_ibias, g_posproj], 1)
    g_packed = lax.all_to_all(g_packed, ALL, split_axis=0, concat_axis=0, tiled=True)
    g_packed = jnp.sum(g_packed.astype(F32), 0)
    s = [g_packed[k, : v.size] for k, v in enumerate(vectors)]
    g_pp = g_packed[n_vec:].reshape(R, DH)

    outer_grad = jnp.concatenate([outer_y.result(), outer_x.result()], 0)

    def by_rows(v):
        v = v.astype(BF).reshape(n_core, R, -1)
        mine = lax.dynamic_index_in_dim(v, core, 0, False)
        other = swap(lax.dynamic_index_in_dim(v, 1 - core, 0, False), "core", 1)
        return jnp.where(core == 0, mine, other), jnp.where(core == 0, other, mine)

    inner_grad = jnp.stack(by_rows(jnp.concatenate([inner_y.result(), inner_x.result()], 1)), 1)
    inner_grad = inner_grad.reshape(R, n_core, 2, chips, U // 2).transpose(0, 3, 1, 2, 4)
    inner_grad = inner_grad.astype(F32).reshape(R, FF)
    out_grad = jnp.concatenate(by_rows(out_y.result()), 1).astype(F32)

    return (
        output, input_grad, g_rows[0], g_rows[1], g_rows[2], out_grad, s[2], s[0], s[1], g_pp,
        s[3], s[4], s[5], inner_grad, s[9], outer_grad, s[6], s[7], s[8],
    )


def solution(mesh):
    n_dp, n_seq = mesh.devices.shape
    mesh = Mesh(mesh.devices.reshape(n_dp // 2, 2, n_seq // 2, 2), ALL)
    tok, ids = P(None, DP, SEQ, None), P(None, DP, SEQ)
    mat, vec = P(ALL, None), P(ALL)
    in_specs = (
        tok, ids, tok, mat, mat, mat, mat, vec, vec, vec, mat, vec, vec, vec, mat, vec, mat, vec,
        vec, vec,
    )
    out_specs = (
        tok, tok, mat, mat, mat, mat, vec, vec, vec, mat, vec, vec, vec, mat, vec, mat, vec, vec,
        vec,
    )
    return jax.shard_map(
        per_device, mesh=mesh, in_specs=in_specs, out_specs=out_specs, check_vma=False
    )
```
